256 devices in a mesh: dp: 2 (over x_lo), context: 8 (over z), tensor: 16 (over y, x_hi, core).
Axes of the slice: x: 4 (x_hi: 2, x_lo: 2; x = x_hi * 2 + x_lo), y: 4, z: 8, core: 2. Of those that a mesh axis runs over, the one named last changes fastest.
Arguments:
- activations: bfloat16 [2, 4096, 4096], P('dp', ('context', 'tensor')), may hold values from -60 to 60
- in_weight: bfloat16 [4096, 3, 4096], P('dp', None, 'tensor'), may hold values from -0.09375 to 0.09375
- out_weight: bfloat16 [4096, 4096], P('tensor', 'dp'), may hold values from -0.09375 to 0.09375
- short_filter: float32 [3, 3, 4096], P(None, None, 'tensor'), may hold values from -2 to 2
- mixer_filter: float32 [128, 256], P(None, 'tensor'), may hold values from -0.5 to 0.5
- cotangent: bfloat16 [2, 4096, 4096], P('dp', ('context', 'tensor')), may hold values from -6 to 6
Outputs:
- block_out: bfloat16 [2, 4096, 4096], P('dp', ('context', 'tensor'))
- grad_input: bfloat16 [2, 4096, 4096], P('dp', ('context', 'tensor'))
- grad_in_weight: bfloat16 [4096, 3, 4096], P(('dp', 'context'), None, 'tensor')
- grad_out_weight: bfloat16 [4096, 4096], P('tensor', ('dp', 'context'))
- grad_short: float32 [3, 3, 4096], P(None, None, 'tensor')
- grad_mixer: float32 [128, 256], P(None, 'tensor')
The draws below stay inside these ranges and needn't reach their ends.
All inputs are finite; a program needn't handle non-finite values.
Results may differ from the reference program's by a relative error of at most 0.019.
Values may be sent and summed in bfloat16 or wider, within the bound.
A program may use at most 128 MiB of HBM per device.

```python
import math
import jax
import jax.numpy as jnp
from jax import lax

D = 4096
TOK_CTX = 512
STAP = 3
LTAP = 128
GRP = 16
FILTERS = 256
SEQS = 2
LEN = 4096
N_CONTEXT = 8
N_TENSOR = 16


def draw_activations(key, part):
    key_rows = jax.random.fold_in(key, 11)
    key_cols = jax.random.fold_in(key, 12)
    key_base = jax.random.fold_in(key, 13)
    lo = math.log(0.3)
    hi = math.log(3.0)
    row_scale = jnp.exp(jax.random.uniform(key_rows, (SEQS, LEN, 1), jnp.float32, lo, hi))
    col_scale = jnp.exp(jax.random.uniform(key_cols, (1, 1, D), jnp.float32, lo, hi))
    base = jnp.clip(jax.random.normal(key_base, (SEQS, LEN, D), jnp.float32), -6.0, 6.0)
    values = base * row_scale * col_scale
    return values.astype(jnp.bfloat16)


def level_of(own_key, dims, split, smallest, high):
    def one(dim, blocks):
        steps = jax.random.uniform(jax.random.fold_in(jax.random.fold_in(own_key, 6), dim), (blocks,), jnp.float32, smallest / len(split), high / len(split))
        return jnp.repeat(jnp.exp(steps), dims[dim] // blocks).reshape((-1,) + (1,) * (len(dims) - dim - 1))

    loudness = one(*split[0])
    for cut in split[1:]:
        loudness = loudness * one(*cut)
    return loudness


def centred(key, shape, width, reach, shards=(), held_as=jnp.bfloat16):
    values = jax.random.normal(key, shape, jnp.float32) * width
    if len(shards) > 0:
        values = level_of(key, shape, shards, -0.22, 0.18) * values
    return jnp.clip(values, min=-reach, max=reach).astype(held_as)


def setup_inputs(seed: int = 0) -> dict:
    seeds = jax.random.split(jax.random.key(seed), 7)
    activations = draw_activations(jax.random.fold_in(seeds[6], 71), 0)
    in_weight = centred(seeds[1], (D, 3, D), D ** -0.5, 0.09375, ((0, 2), (2, 16)))
    out_weight = centred(seeds[2], (D, D), D ** -0.5, 0.09375, ((0, 16), (1, 2)))
    short_filter = centred(seeds[3], (3, STAP, D), 0.4, 2.0, ((2, 16),), jnp.float32)
    mixer_filter = centred(seeds[4], (LTAP, FILTERS), 0.09, 0.5, ((1, 16),), jnp.float32)
    cotangent = centred(seeds[5], (SEQS, LEN, D), 1.0, 6.0, ((0, 2), (1, 128)))
    return dict(activations=activations, in_weight=in_weight, out_weight=out_weight, short_filter=short_filter, mixer_filter=mixer_filter, cotangent=cotangent)


EPS = 1e-05

def roundtrip(value):
    return lax.optimization_barrier(value.astype(jnp.bfloat16)).astype(jnp.float32)

def mix_forward(gate_pad, filt):

    def step(tap, acc):
        start = (LTAP - 1 - tap).astype(jnp.int32)
        return acc + filt[tap][None, :] * lax.dynamic_slice_in_dim(gate_pad, start, LEN, 0)
    return lax.fori_loop(0, LTAP, step, jnp.zeros((LEN, D), jnp.float32))

def mix_backward(grad_pad, filt):

    def step(tap, acc):
        start = jnp.asarray(tap).astype(jnp.int32)
        return acc + filt[tap][None, :] * lax.dynamic_slice_in_dim(grad_pad, start, LEN, 0)
    return lax.fori_loop(0, LTAP, step, jnp.zeros((LEN, D), jnp.float32))

def reference(activations, in_weight, out_weight, short_filter, mixer_filter, cotangent):
    chans = D // N_TENSOR
    mixer_full = jnp.repeat(mixer_filter, GRP, axis=1)
    in_flat = in_weight.reshape(D, 3 * D)
    outs = []
    grads = []
    grad_in_total = jnp.zeros((D, 3 * D), jnp.float32)
    grad_out_total = jnp.zeros((D, D), jnp.float32)
    grad_short = jnp.zeros((3, STAP, D), jnp.float32)
    grad_mixer = jnp.zeros((LTAP, D // GRP), jnp.float32)
    for seq in range(SEQS):
        rowvals = activations[seq].astype(jnp.float32)
        inverse = lax.rsqrt(lax.optimization_barrier(jnp.mean(rowvals * rowvals, axis=-1, keepdims=True)) + EPS)
        normed = (rowvals * inverse).astype(jnp.bfloat16)
        projected = jnp.dot(normed, in_flat, preferred_element_type=jnp.float32).astype(jnp.bfloat16).reshape(LEN, 3, D)
        proj_pad = jnp.concatenate([jnp.zeros((STAP - 1, 3, D), jnp.float32), projected.astype(jnp.float32)], 0)
        streams = jnp.zeros((LEN, 3, D), jnp.float32)
        for tap in range(STAP):
            streams = streams + short_filter[:, tap][None] * proj_pad[STAP - 1 - tap:STAP - 1 - tap + LEN]
        gated = (streams[:, 1] * streams[:, 2]).astype(jnp.bfloat16)
        gate_pad = jnp.concatenate([jnp.zeros((LTAP - 1, D), jnp.float32), gated.astype(jnp.float32)], 0)
        mixed = mix_forward(gate_pad, mixer_full)
        output_rows = (streams[:, 0] * mixed).astype(jnp.bfloat16)
        branch = jnp.zeros((LEN, D), jnp.float32)
        for group in range(N_TENSOR):
            lo = group * chans
            branch = branch + roundtrip(jnp.dot(output_rows[:, lo:lo + chans], out_weight[lo:lo + chans], preferred_element_type=jnp.float32))
        outs.append((rowvals + branch).astype(jnp.bfloat16))
        cot = cotangent[seq]
        grad_rows = jnp.dot(cot, out_weight.T, preferred_element_type=jnp.float32)
        for block in range(N_CONTEXT):
            lo = block * TOK_CTX
            grad_out_total = grad_out_total + roundtrip(jnp.dot(output_rows[lo:lo + TOK_CTX].T, cot[lo:lo + TOK_CTX], preferred_element_type=jnp.float32))
        grad_mix = (grad_rows * streams[:, 0]).astype(jnp.bfloat16)
        grad_mix_wide = grad_mix.astype(jnp.float32)
        grad_pad = jnp.concatenate([grad_mix_wide, jnp.zeros((LTAP - 1, D), jnp.float32)], 0)
        grad_gate = mix_backward(grad_pad, mixer_full)

        def tap_grad(tap):
            start = (LTAP - 1 - tap).astype(jnp.int32)
            return lax.optimization_barrier(jnp.sum(grad_mix_wide * lax.dynamic_slice_in_dim(gate_pad, start, LEN, 0), axis=0))
        per_tap = lax.map(tap_grad, jnp.arange(LTAP))
        grad_mixer = grad_mixer + per_tap.reshape(LTAP, D // GRP, GRP).sum(axis=-1)
        grad_streams = jnp.stack([grad_rows * mixed, grad_gate * streams[:, 2], grad_gate * streams[:, 1]], axis=1)
        stream_pad = jnp.concatenate([grad_streams, jnp.zeros((STAP - 1, 3, D), jnp.float32)], 0)
        grad_proj = jnp.zeros((LEN, 3, D), jnp.float32)
        for tap in range(STAP):
            grad_proj = grad_proj + short_filter[:, tap][None] * stream_pad[tap:tap + LEN]
        grad_proj = grad_proj.astype(jnp.bfloat16)
        short_terms = [lax.optimization_barrier(jnp.sum(grad_streams * proj_pad[STAP - 1 - tap:STAP - 1 - tap + LEN], axis=0)) for tap in range(STAP)]
        grad_short = grad_short + jnp.stack(short_terms, axis=1)
        proj_flat = grad_proj.reshape(LEN, 3 * D)
        for block in range(N_CONTEXT):
            lo = block * TOK_CTX
            grad_in_total = grad_in_total + roundtrip(jnp.dot(normed[lo:lo + TOK_CTX].T, proj_flat[lo:lo + TOK_CTX], preferred_element_type=jnp.float32))
        grad_norm = jnp.zeros((LEN, D), jnp.float32)
        for group in range(N_TENSOR):
            lo = group * chans
            piece = grad_proj[:, :, lo:lo + chans].reshape(LEN, 3 * chans)
            weights = in_weight[:, :, lo:lo + chans].reshape(D, 3 * chans)
            grad_norm = grad_norm + roundtrip(lax.dot_general(piece, weights, (((1,), (1,)), ((), ())), preferred_element_type=jnp.float32))
        grad_x = cot.astype(jnp.float32) + inverse * grad_norm - rowvals * inverse ** 3 * lax.optimization_barrier(jnp.mean(grad_norm * rowvals, axis=-1, keepdims=True))
        grads.append(grad_x.astype(jnp.bfloat16))
    block_out = jnp.stack(outs, 0)
    grad_input = jnp.stack(grads, 0)
    return (block_out, grad_input, grad_in_total.reshape(D, 3, D).astype(jnp.bfloat16), grad_out_total.astype(jnp.bfloat16), grad_short, grad_mixer)
```

```python
import jax
import jax.numpy as jnp
from jax import lax
from jax.sharding import PartitionSpec as P

EPS = 1e-05


def from_behind(value, axis, steps):
    count = lax.axis_size(axis)
    initial, last = (max(0, -steps), min(count, count - steps))
    return lax.ppermute(value, axis, [(source, source + steps) for source in range(initial, last)])


def pair_gather(value, axis, dim):
    count = lax.axis_size(axis)
    index = lax.axis_index(axis)
    parts = [value]
    for step in range(1, count):
        parts.append(lax.ppermute(value, axis, [(i, (i + step) % count) for i in range(count)]))
    shape = list(value.shape)
    size = shape[dim]
    shape[dim] = size * count
    full = jnp.zeros(shape, value.dtype)
    for step, part in enumerate(parts):
        start = [0] * len(shape)
        start[dim] = ((index - step) % count) * size
        full = lax.dynamic_update_slice(full, part, start)
    return full


def scatter_sum(value, axis, dim):
    count = lax.axis_size(axis)
    shape = value.shape
    split = shape[:dim] + (count, shape[dim] // count) + shape[dim + 1 :]
    pieces = lax.all_to_all(value.reshape(split), axis, dim, 0)
    return jnp.sum(pieces.astype(jnp.float32), axis=0)


def skew_table(base, span):
    groups = base.shape[0]
    padded = jnp.concatenate([base, jnp.zeros((groups, span + 1), jnp.float32)], axis=1)
    tiled = jnp.tile(padded[:, None, :], (1, span, 1)).reshape(groups, span * (2 * span + 1))
    return tiled[:, : span * 2 * span].reshape(groups, span, 2 * span)


def band_windows(extended, span, groups):
    chans = extended.shape[1]
    padded = jnp.concatenate([extended, jnp.zeros((1, chans), jnp.float32)], 0)
    blocks = padded.shape[0] // span
    padded = padded.reshape(blocks, span, groups, chans // groups)
    return jnp.concatenate([padded[:-1], padded[1:]], axis=1)


def band_apply(table, extended, span):
    groups = table.shape[0]
    chans = extended.shape[1]
    windows = band_windows(extended, span, groups)
    result = jnp.einsum("gtu,bugc->btgc", table, windows, precision=lax.Precision.HIGHEST)
    return result.reshape(windows.shape[0] * span, chans)


def band_grad(left, extended, span, groups):
    rows, chans = left.shape
    lhs = left.reshape(rows // span, span, groups, chans // groups)
    windows = band_windows(extended, span, groups)
    prods = jnp.einsum("btgc,bugc->gtu", lhs, windows, precision=lax.Precision.HIGHEST)
    flat = jnp.concatenate(
        [prods.reshape(groups, span * 2 * span), jnp.zeros((groups, span), jnp.float32)], axis=1
    )
    skewed = flat.reshape(groups, span, 2 * span + 1).sum(axis=1)
    return jnp.flip(skewed[:, :span], axis=1).T


def short_apply(filters, extended, rows):
    taps = filters.shape[1]
    total = jnp.zeros((rows,) + extended.shape[1:], jnp.float32)
    for tap in range(taps):
        total = total + filters[:, tap][None] * extended[taps - 1 - tap : taps - 1 - tap + rows]
    return total


def per_device(activations, in_weight, out_weight, short_filter, mixer_filter, cotangent):
    rows_own = activations.shape[1]
    width = activations.shape[2]
    rows = rows_own * lax.axis_size("tensor")
    span = mixer_filter.shape[0]
    groups = mixer_filter.shape[1]
    taps = short_filter.shape[1]
    chans = short_filter.shape[2]
    own = activations[0].astype(jnp.float32)
    inverse = lax.rsqrt(jnp.mean(own * own, axis=-1, keepdims=True) + EPS)
    normed = (own * inverse).astype(jnp.bfloat16)
    slab = lax.all_gather(normed, "tensor", axis=0, tiled=True)
    full_in = pair_gather(in_weight, "dp", 0)
    full_out = pair_gather(out_weight, "dp", 1)
    in_flat = full_in.reshape(width, 3 * chans)
    projected = (
        jnp.dot(slab, in_flat, preferred_element_type=jnp.float32)
        .astype(jnp.bfloat16)
        .reshape(rows, 3, chans)
    )
    proj_wide = projected.astype(jnp.float32)
    table_fwd = skew_table(jnp.flip(mixer_filter, axis=0).T, span)
    table_back = skew_table(mixer_filter.T, span)
    short_rim = from_behind(projected[rows - taps + 1 :], "context", 1)
    proj_ext = jnp.concatenate([short_rim.astype(jnp.float32), proj_wide], 0)
    streams = short_apply(short_filter, proj_ext, rows)
    gated = (streams[:, 1] * streams[:, 2]).astype(jnp.bfloat16)
    gate_rim = from_behind(gated[rows - span + 1 :], "context", 1)
    gate_ext = jnp.concatenate([gate_rim, gated], 0).astype(jnp.float32)
    mixed = band_apply(table_fwd, gate_ext, span)
    output_rows = (streams[:, 0] * mixed).astype(jnp.bfloat16)
    piece = output_rows
    branch = scatter_sum(
        jnp.dot(piece, full_out, preferred_element_type=jnp.float32).astype(jnp.bfloat16),
        "tensor",
        0,
    )
    block_out = (own + branch).astype(jnp.bfloat16)[None]
    cot_slab = lax.all_gather(cotangent[0], "tensor", axis=0, tiled=True)
    grad_rows = lax.dot_general(
        cot_slab, full_out, (((1,), (1,)), ((), ())), preferred_element_type=jnp.float32
    )
    out_term = lax.dot_general(
        output_rows, cot_slab, (((0,), (0,)), ((), ())), preferred_element_type=jnp.float32
    )
    grad_mix = (grad_rows * streams[:, 0]).astype(jnp.bfloat16)
    grad_mix_wide = grad_mix.astype(jnp.float32)
    mix_rim = from_behind(grad_mix[: span - 1], "context", -1)
    grad_gate = band_apply(
        table_back, jnp.concatenate([grad_mix_wide, mix_rim.astype(jnp.float32)], 0), span
    )
    mixer_term = band_grad(grad_mix_wide, gate_ext, span, groups)
    grad_streams = jnp.stack(
        [grad_rows * mixed, grad_gate * streams[:, 2], grad_gate * streams[:, 1]], axis=1
    )
    stream_rim = from_behind(grad_streams[: taps - 1], "context", -1)
    stream_ext = jnp.concatenate([grad_streams, stream_rim], 0)
    grad_proj = jnp.zeros((rows, 3, chans), jnp.float32)
    for tap in range(taps):
        grad_proj = grad_proj + short_filter[:, tap][None] * stream_ext[tap : tap + rows]
    grad_proj = grad_proj.astype(jnp.bfloat16)
    short_terms = [
        jnp.sum(grad_streams * proj_ext[taps - 1 - tap : taps - 1 - tap + rows], axis=0)
        for tap in range(taps)
    ]
    short_term = jnp.stack(short_terms, axis=1)
    grad_short, grad_mixer = lax.psum((short_term, mixer_term), ("dp", "context"))
    proj_flat = grad_proj.reshape(rows, 3 * chans)
    in_term = lax.dot_general(
        slab, proj_flat, (((0,), (0,)), ((), ())), preferred_element_type=jnp.float32
    ).reshape(width, 3, chans)
    grad_in, grad_out = (
        lax.psum_scatter(
            in_term.astype(jnp.bfloat16), ("dp", "context"), scatter_dimension=0, tiled=True
        ).astype(jnp.float32),
        lax.psum_scatter(
            out_term.astype(jnp.bfloat16), ("dp", "context"), scatter_dimension=1, tiled=True
        ).astype(jnp.float32),
    )
    piece = proj_flat
    grad_norm = scatter_sum(
        lax.dot_general(
            piece, in_flat, (((1,), (1,)), ((), ())), preferred_element_type=jnp.float32
        ).astype(jnp.bfloat16),
        "tensor",
        0,
    )
    grad_x = (
        cotangent[0].astype(jnp.float32)
        + inverse * grad_norm
        - own * inverse**3 * jnp.mean(grad_norm * own, axis=-1, keepdims=True)
    )
    grad_input = grad_x.astype(jnp.bfloat16)[None]
    return (
        block_out,
        grad_input,
        grad_in.astype(jnp.bfloat16),
        grad_out.astype(jnp.bfloat16),
        grad_short,
        grad_mixer,
    )


def solution(mesh):
    placed = (
        P("dp", ("context", "tensor"), None),
        P("dp", None, "tensor"),
        P("tensor", "dp"),
        P(None, None, "tensor"),
        P(None, "tensor"),
        P("dp", ("context", "tensor"), None),
    )
    return jax.shard_map(
        per_device,
        mesh=mesh,
        in_specs=placed,
        out_specs=(
            P("dp", ("context", "tensor"), None),
            P("dp", ("context", "tensor"), None),
            P(("dp", "context"), None, "tensor"),
            P("tensor", ("dp", "context")),
            P(None, None, "tensor"),
            P(None, "tensor"),
        ),
        check_vma=False,
    )
```

```python
import jax
import jax.numpy as jnp
from jax import lax
from jax.sharding import PartitionSpec as P

EPS = 1e-05


def from_behind(value, axis, steps):
    count = lax.axis_size(axis)
    initial, last = (max(0, -steps), min(count, count - steps))
    return lax.ppermute(value, axis, [(source, source + steps) for source in range(initial, last)])


def pair_gather(value, axis, dim):
    count = lax.axis_size(axis)
    index = lax.axis_index(axis)
    parts = [value]
    for step in range(1, count):
        parts.append(lax.ppermute(value, axis, [(i, (i + step) % count) for i in range(count)]))
    shape = list(value.shape)
    size = shape[dim]
    shape[dim] = size * count
    full = jnp.zeros(shape, value.dtype)
    for step, part in enumerate(parts):
        start = [0] * len(shape)
        start[dim] = ((index - step) % count) * size
        full = lax.dynamic_update_slice(full, part, start)
    return full


def tree_psum(value, axes):
    for axis in axes:
        count = lax.axis_size(axis)
        if count & (count - 1):
            value = lax.psum(value, axis)
            continue
        step = 1
        while step < count:
            partner = lax.ppermute(value, axis, [(i, i ^ step) for i in range(count)])
            value = value + partner
            step *= 2
    return value


def scatter_sum(value, axis, dim):
    count = lax.axis_size(axis)
    shape = value.shape
    split = shape[:dim] + (count, shape[dim] // count) + shape[dim + 1 :]
    pieces = lax.all_to_all(value.reshape(split), axis, dim, 0)
    return jnp.sum(pieces.astype(jnp.float32), axis=0)


def skew_table(base, span):
    groups = base.shape[0]
    padded = jnp.concatenate([base, jnp.zeros((groups, span + 1), jnp.float32)], axis=1)
    tiled = jnp.tile(padded[:, None, :], (1, span, 1)).reshape(groups, span * (2 * span + 1))
    return tiled[:, : span * 2 * span].reshape(groups, span, 2 * span)


def band_windows(extended, span, groups):
    chans = extended.shape[1]
    padded = jnp.concatenate([extended, jnp.zeros((1, chans), jnp.float32)], 0)
    blocks = padded.shape[0] // span
    padded = padded.reshape(blocks, span, groups, chans // groups)
    return jnp.concatenate([padded[:-1], padded[1:]], axis=1)


def band_apply(table, extended, span):
    groups = table.shape[0]
    chans = extended.shape[1]
    windows = band_windows(extended, span, groups).astype(jnp.bfloat16)
    high = table.astype(jnp.bfloat16)
    low = (table - high.astype(jnp.float32)).astype(jnp.bfloat16)
    result = jnp.einsum(
        "gtu,bugc->btgc", high, windows, preferred_element_type=jnp.float32
    ) + jnp.einsum("gtu,bugc->btgc", low, windows, preferred_element_type=jnp.float32)
    return result.reshape(windows.shape[0] * span, chans)


def band_grad(left, extended, span, groups):
    rows, chans = left.shape
    lhs = left.reshape(rows // span, span, groups, chans // groups)
    windows = band_windows(extended, span, groups).astype(jnp.bfloat16)
    prods = jnp.einsum(
        "btgc,bugc->gtu", lhs.astype(jnp.bfloat16), windows, preferred_element_type=jnp.float32
    )
    flat = jnp.concatenate(
        [prods.reshape(groups, span * 2 * span), jnp.zeros((groups, span), jnp.float32)], axis=1
    )
    skewed = flat.reshape(groups, span, 2 * span + 1).sum(axis=1)
    return jnp.flip(skewed[:, :span], axis=1).T


def short_apply(filters, extended, rows):
    taps = filters.shape[1]
    total = jnp.zeros((rows,) + extended.shape[1:], jnp.float32)
    for tap in range(taps):
        total = total + filters[:, tap][None] * extended[taps - 1 - tap : taps - 1 - tap + rows]
    return total


def per_device(activations, in_weight, out_weight, short_filter, mixer_filter, cotangent):
    rows_own = activations.shape[1]
    width = activations.shape[2]
    rows = rows_own * lax.axis_size("tensor")
    span = mixer_filter.shape[0]
    groups = mixer_filter.shape[1]
    taps = short_filter.shape[1]
    chans = short_filter.shape[2]
    own = activations[0].astype(jnp.float32)
    inverse = lax.rsqrt(jnp.mean(own * own, axis=-1, keepdims=True) + EPS)
    normed = (own * inverse).astype(jnp.bfloat16)
    slab = lax.all_gather(normed, "tensor", axis=0, tiled=True)
    full_in = pair_gather(in_weight, "dp", 0)
    full_out = pair_gather(out_weight, "dp", 1)
    in_flat = full_in.reshape(width, 3 * chans)
    projected = (
        jnp.dot(slab, in_flat, preferred_element_type=jnp.float32)
        .astype(jnp.bfloat16)
        .reshape(rows, 3, chans)
    )
    proj_wide = projected.astype(jnp.float32)
    table_fwd = skew_table(jnp.flip(mixer_filter, axis=0).T, span)
    table_back = skew_table(mixer_filter.T, span)
    short_rim = from_behind(projected[rows - taps + 1 :], "context", 1)
    proj_ext = jnp.concatenate([short_rim.astype(jnp.float32), proj_wide], 0)
    streams = short_apply(short_filter, proj_ext, rows)
    gated = (streams[:, 1] * streams[:, 2]).astype(jnp.bfloat16)
    gate_rim = from_behind(gated[rows - span + 1 :], "context", 1)
    gate_ext = jnp.concatenate([gate_rim, gated], 0).astype(jnp.float32)
    mixed = band_apply(table_fwd, gate_ext, span)
    output_rows = (streams[:, 0] * mixed).astype(jnp.bfloat16)
    piece = output_rows
    branch = scatter_sum(
        jnp.dot(piece, full_out, preferred_element_type=jnp.float32).astype(jnp.bfloat16),
        "tensor",
        0,
    )
    block_out = (own + branch).astype(jnp.bfloat16)[None]
    cot_slab = lax.all_gather(cotangent[0], "tensor", axis=0, tiled=True)
    grad_rows = lax.dot_general(
        cot_slab, full_out, (((1,), (1,)), ((), ())), preferred_element_type=jnp.float32
    )
    out_term = lax.dot_general(
        output_rows, cot_slab, (((0,), (0,)), ((), ())), preferred_element_type=jnp.float32
    )
    grad_mix = (grad_rows * streams[:, 0]).astype(jnp.bfloat16)
    grad_mix_wide = grad_mix.astype(jnp.float32)
    mix_rim = from_behind(grad_mix[: span - 1], "context", -1)
    grad_gate = band_apply(
        table_back, jnp.concatenate([grad_mix_wide, mix_rim.astype(jnp.float32)], 0), span
    )
    mixer_term = band_grad(grad_mix_wide, gate_ext, span, groups)
    grad_streams = jnp.stack(
        [grad_rows * mixed, grad_gate * streams[:, 2], grad_gate * streams[:, 1]], axis=1
    )
    stream_rim = from_behind(grad_streams[: taps - 1], "context", -1)
    stream_ext = jnp.concatenate([grad_streams, stream_rim], 0)
    grad_proj = jnp.zeros((rows, 3, chans), jnp.float32)
    for tap in range(taps):
        grad_proj = grad_proj + short_filter[:, tap][None] * stream_ext[tap : tap + rows]
    grad_proj = grad_proj.astype(jnp.bfloat16)
    short_terms = [
        jnp.sum(grad_streams * proj_ext[taps - 1 - tap : taps - 1 - tap + rows], axis=0)
        for tap in range(taps)
    ]
    short_term = jnp.stack(short_terms, axis=1)
    flat = tree_psum(jnp.concatenate([short_term.ravel(), mixer_term.ravel()]), ("dp", "context"))
    grad_short = flat[: short_term.size].reshape(short_term.shape)
    grad_mixer = flat[short_term.size :].reshape(mixer_term.shape)
    proj_flat = grad_proj.reshape(rows, 3 * chans)
    in_term = lax.dot_general(
        slab, proj_flat, (((0,), (0,)), ((), ())), preferred_element_type=jnp.float32
    ).reshape(width, 3, chans)
    grad_in, grad_out = (
        lax.psum_scatter(
            in_term.astype(jnp.bfloat16), ("dp", "context"), scatter_dimension=0, tiled=True
        ).astype(jnp.float32),
        lax.psum_scatter(
            out_term.astype(jnp.bfloat16), ("dp", "context"), scatter_dimension=1, tiled=True
        ).astype(jnp.float32),
    )
    piece = proj_flat
    grad_norm = scatter_sum(
        lax.dot_general(
            piece, in_flat, (((1,), (1,)), ((), ())), preferred_element_type=jnp.float32
        ).astype(jnp.bfloat16),
        "tensor",
        0,
    )
    grad_x = (
        cotangent[0].astype(jnp.float32)
        + inverse * grad_norm
        - own * inverse**3 * jnp.mean(grad_norm * own, axis=-1, keepdims=True)
    )
    grad_input = grad_x.astype(jnp.bfloat16)[None]
    return (
        block_out,
        grad_input,
        grad_in.astype(jnp.bfloat16),
        grad_out.astype(jnp.bfloat16),
        grad_short,
        grad_mixer,
    )


def solution(mesh):
    placed = (
        P("dp", ("context", "tensor"), None),
        P("dp", None, "tensor"),
        P("tensor", "dp"),
        P(None, None, "tensor"),
        P(None, "tensor"),
        P("dp", ("context", "tensor"), None),
    )
    return jax.shard_map(
        per_device,
        mesh=mesh,
        in_specs=placed,
        out_specs=(
            P("dp", ("context", "tensor"), None),
            P("dp", ("context", "tensor"), None),
            P(("dp", "context"), None, "tensor"),
            P("tensor", ("dp", "context")),
            P(None, None, "tensor"),
            P(None, "tensor"),
        ),
        check_vma=False,
    )
```

```python
import jax
import jax.numpy as jnp
from jax import lax
from jax.sharding import PartitionSpec as P

EPS = 1e-05
TENSOR = ("tchip", "core")


def from_behind(value, axis, steps):
    count = lax.axis_size(axis)
    initial, last = (max(0, -steps), min(count, count - steps))
    return lax.ppermute(value, axis, [(source, source + steps) for source in range(initial, last)])


def pair_gather(value, axis, dim):
    count = lax.axis_size(axis)
    index = lax.axis_index(axis)
    parts = [value]
    for step in range(1, count):
        parts.append(lax.ppermute(value, axis, [(i, (i + step) % count) for i in range(count)]))
    shape = list(value.shape)
    size = shape[dim]
    shape[dim] = size * count
    full = jnp.zeros(shape, value.dtype)
    for step, part in enumerate(parts):
        start = [0] * len(shape)
        start[dim] = ((index - step) % count) * size
        full = lax.dynamic_update_slice(full, part, start)
    return full


def tree_psum(value, axes):
    for axis in axes:
        count = lax.axis_size(axis)
        if count & (count - 1):
            value = lax.psum(value, axis)
            continue
        step = 1
        while step < count:
            partner = lax.ppermute(value, axis, [(i, i ^ step) for i in range(count)])
            value = value + partner
            step *= 2
    return value


def pair_scatter_sum(value):
    chips = lax.axis_size("tchip")
    cores = lax.axis_size("core")
    rows, width = value.shape
    value = value.reshape(chips, cores, rows // (chips * cores), width)
    pieces = lax.all_to_all(value, "core", 1, 1)
    paired = jnp.sum(pieces.astype(jnp.float32), axis=1).astype(jnp.bfloat16)
    pieces = lax.all_to_all(paired, "tchip", 0, 0)
    return jnp.sum(pieces.astype(jnp.float32), axis=0)


def scatter_sum(value, axis, dim):
    count = lax.axis_size(axis)
    shape = value.shape
    split = shape[:dim] + (count, shape[dim] // count) + shape[dim + 1 :]
    pieces = lax.all_to_all(value.reshape(split), axis, dim, 0)
    return jnp.sum(pieces.astype(jnp.float32), axis=0)


def skew_table(base, span):
    groups = base.shape[0]
    padded = jnp.concatenate([base, jnp.zeros((groups, span + 1), jnp.float32)], axis=1)
    tiled = jnp.tile(padded[:, None, :], (1, span, 1)).reshape(groups, span * (2 * span + 1))
    return tiled[:, : span * 2 * span].reshape(groups, span, 2 * span)


def band_windows(extended, span, groups):
    chans = extended.shape[1]
    padded = jnp.concatenate([extended, jnp.zeros((1, chans), jnp.float32)], 0)
    blocks = padded.shape[0] // span
    padded = padded.reshape(blocks, span, groups, chans // groups)
    return jnp.concatenate([padded[:-1], padded[1:]], axis=1)


def band_apply(table, extended, span):
    groups = table.shape[0]
    chans = extended.shape[1]
    windows = band_windows(extended, span, groups).astype(jnp.bfloat16)
    high = table.astype(jnp.bfloat16)
    low = (table - high.astype(jnp.float32)).astype(jnp.bfloat16)
    result = jnp.einsum(
        "gtu,bugc->btgc", high, windows, preferred_element_type=jnp.float32
    ) + jnp.einsum("gtu,bugc->btgc", low, windows, preferred_element_type=jnp.float32)
    return result.reshape(windows.shape[0] * span, chans)


def band_grad(left, extended, span, groups):
    rows, chans = left.shape
    lhs = left.reshape(rows // span, span, groups, chans // groups)
    windows = band_windows(extended, span, groups).astype(jnp.bfloat16)
    prods = jnp.einsum(
        "btgc,bugc->gtu", lhs.astype(jnp.bfloat16), windows, preferred_element_type=jnp.float32
    )
    flat = jnp.concatenate(
        [prods.reshape(groups, span * 2 * span), jnp.zeros((groups, span), jnp.float32)], axis=1
    )
    skewed = flat.reshape(groups, span, 2 * span + 1).sum(axis=1)
    return jnp.flip(skewed[:, :span], axis=1).T


def short_apply(filters, extended, rows):
    taps = filters.shape[1]
    total = jnp.zeros((rows,) + extended.shape[1:], jnp.float32)
    for tap in range(taps):
        total = total + filters[:, tap][None] * extended[taps - 1 - tap : taps - 1 - tap + rows]
    return total


def per_device(activations, in_weight, out_weight, short_filter, mixer_filter, cotangent):
    rows_own = activations.shape[1]
    width = activations.shape[2]
    rows = rows_own * lax.axis_size("tchip") * lax.axis_size("core")
    span = mixer_filter.shape[0]
    groups = mixer_filter.shape[1]
    taps = short_filter.shape[1]
    chans = short_filter.shape[2]
    own = activations[0].astype(jnp.float32)
    inverse = lax.rsqrt(jnp.mean(own * own, axis=-1, keepdims=True) + EPS)
    normed = (own * inverse).astype(jnp.bfloat16)
    slab = lax.all_gather(normed, TENSOR, axis=0, tiled=True)
    full_in = pair_gather(in_weight, "dp", 0)
    full_out = pair_gather(out_weight, "dp", 1)
    in_flat = full_in.reshape(width, 3 * chans)
    projected = (
        jnp.dot(slab, in_flat, preferred_element_type=jnp.float32)
        .astype(jnp.bfloat16)
        .reshape(rows, 3, chans)
    )
    proj_wide = projected.astype(jnp.float32)
    table_fwd = skew_table(jnp.flip(mixer_filter, axis=0).T, span)
    table_back = skew_table(mixer_filter.T, span)
    short_rim = from_behind(projected[rows - taps + 1 :], "context", 1)
    proj_ext = jnp.concatenate([short_rim.astype(jnp.float32), proj_wide], 0)
    streams = short_apply(short_filter, proj_ext, rows)
    gated = (streams[:, 1] * streams[:, 2]).astype(jnp.bfloat16)
    gate_rim = from_behind(gated[rows - span + 1 :], "context", 1)
    gate_ext = jnp.concatenate([gate_rim, gated], 0).astype(jnp.float32)
    mixed = band_apply(table_fwd, gate_ext, span)
    output_rows = (streams[:, 0] * mixed).astype(jnp.bfloat16)
    piece = output_rows
    branch = pair_scatter_sum(
        jnp.dot(piece, full_out, preferred_element_type=jnp.float32).astype(jnp.bfloat16)
    )
    block_out = (own + branch).astype(jnp.bfloat16)[None]
    cot_slab = lax.all_gather(cotangent[0], TENSOR, axis=0, tiled=True)
    grad_rows = lax.dot_general(
        cot_slab, full_out, (((1,), (1,)), ((), ())), preferred_element_type=jnp.float32
    )
    out_term = lax.dot_general(
        output_rows, cot_slab, (((0,), (0,)), ((), ())), preferred_element_type=jnp.float32
    )
    grad_mix = (grad_rows * streams[:, 0]).astype(jnp.bfloat16)
    grad_mix_wide = grad_mix.astype(jnp.float32)
    mix_rim = from_behind(grad_mix[: span - 1], "context", -1)
    grad_gate = band_apply(
        table_back, jnp.concatenate([grad_mix_wide, mix_rim.astype(jnp.float32)], 0), span
    )
    mixer_term = band_grad(grad_mix_wide, gate_ext, span, groups)
    grad_streams = jnp.stack(
        [grad_rows * mixed, grad_gate * streams[:, 2], grad_gate * streams[:, 1]], axis=1
    )
    stream_rim = from_behind(grad_streams[: taps - 1], "context", -1)
    stream_ext = jnp.concatenate([grad_streams, stream_rim], 0)
    grad_proj = jnp.zeros((rows, 3, chans), jnp.float32)
    for tap in range(taps):
        grad_proj = grad_proj + short_filter[:, tap][None] * stream_ext[tap : tap + rows]
    grad_proj = grad_proj.astype(jnp.bfloat16)
    short_terms = [
        jnp.sum(grad_streams * proj_ext[taps - 1 - tap : taps - 1 - tap + rows], axis=0)
        for tap in range(taps)
    ]
    short_term = jnp.stack(short_terms, axis=1)
    flat = tree_psum(jnp.concatenate([short_term.ravel(), mixer_term.ravel()]), ("dp", "context"))
    grad_short = flat[: short_term.size].reshape(short_term.shape)
    grad_mixer = flat[short_term.size :].reshape(mixer_term.shape)
    proj_flat = grad_proj.reshape(rows, 3 * chans)
    in_term = lax.dot_general(
        slab, proj_flat, (((0,), (0,)), ((), ())), preferred_element_type=jnp.float32
    ).reshape(width, 3, chans)
    grad_in, grad_out = (
        lax.psum_scatter(
            in_term.astype(jnp.bfloat16), ("dp", "context"), scatter_dimension=0, tiled=True
        ).astype(jnp.float32),
        lax.psum_scatter(
            out_term.astype(jnp.bfloat16), ("dp", "context"), scatter_dimension=1, tiled=True
        ).astype(jnp.float32),
    )
    piece = proj_flat
    grad_norm = pair_scatter_sum(
        lax.dot_general(
            piece, in_flat, (((1,), (1,)), ((), ())), preferred_element_type=jnp.float32
        ).astype(jnp.bfloat16)
    )
    grad_x = (
        cotangent[0].astype(jnp.float32)
        + inverse * grad_norm
        - own * inverse**3 * jnp.mean(grad_norm * own, axis=-1, keepdims=True)
    )
    grad_input = grad_x.astype(jnp.bfloat16)[None]
    return (
        block_out,
        grad_input,
        grad_in.astype(jnp.bfloat16),
        grad_out.astype(jnp.bfloat16),
        grad_short,
        grad_mixer,
    )


def solution(mesh):
    devices = mesh.devices
    lead = devices.shape[:2]
    cores = 2
    chips = devices.shape[2] // cores
    mesh = jax.sharding.Mesh(
        devices.reshape(lead + (chips, cores)), ("dp", "context", "tchip", "core")
    )
    placed = (
        P("dp", ("context", "tchip", "core"), None),
        P("dp", None, TENSOR),
        P(TENSOR, "dp"),
        P(None, None, TENSOR),
        P(None, TENSOR),
        P("dp", ("context", "tchip", "core"), None),
    )
    return jax.shard_map(
        per_device,
        mesh=mesh,
        in_specs=placed,
        out_specs=(
            P("dp", ("context", "tchip", "core"), None),
            P("dp", ("context", "tchip", "core"), None),
            P(("dp", "context"), None, TENSOR),
            P(TENSOR, ("dp", "context")),
            P(None, None, TENSOR),
            P(None, TENSOR),
        ),
        check_vma=False,
    )
```

```python
import jax
import jax.numpy as jnp
from jax import lax
from jax.sharding import PartitionSpec as P

EPS = 1e-05
TENSOR = ("tchip", "core")


def from_behind(value, axis, steps):
    count = lax.axis_size(axis)
    initial, last = (max(0, -steps), min(count, count - steps))
    return lax.ppermute(value, axis, [(source, source + steps) for source in range(initial, last)])


def pair_gather(value, axis, dim):
    count = lax.axis_size(axis)
    index = lax.axis_index(axis)
    parts = [value]
    for step in range(1, count):
        parts.append(lax.ppermute(value, axis, [(i, (i + step) % count) for i in range(count)]))
    shape = list(value.shape)
    size = shape[dim]
    shape[dim] = size * count
    full = jnp.zeros(shape, value.dtype)
    for step, part in enumerate(parts):
        start = [0] * len(shape)
        start[dim] = ((index - step) % count) * size
        full = lax.dynamic_update_slice(full, part, start)
    return full


def tree_psum(value, axes):
    for axis in axes:
        count = lax.axis_size(axis)
        if count & (count - 1):
            value = lax.psum(value, axis)
            continue
        step = 1
        while step < count:
            partner = lax.ppermute(value, axis, [(i, i ^ step) for i in range(count)])
            value = value + partner
            step *= 2
    return value


def pair_scatter_sum(value):
    chips = lax.axis_size("tchip")
    cores = lax.axis_size("core")
    rows, width = value.shape
    value = value.reshape(chips, cores, rows // (chips * cores), width)
    pieces = lax.all_to_all(value, "core", 1, 1)
    paired = jnp.sum(pieces.astype(jnp.float32), axis=1).astype(jnp.bfloat16)
    pieces = lax.all_to_all(paired, "tchip", 0, 0)
    return jnp.sum(pieces.astype(jnp.float32), axis=0)


def scatter_sum(value, axis, dim):
    count = lax.axis_size(axis)
    shape = value.shape
    split = shape[:dim] + (count, shape[dim] // count) + shape[dim + 1 :]
    pieces = lax.all_to_all(value.reshape(split), axis, dim, 0)
    return jnp.sum(pieces.astype(jnp.float32), axis=0)


def skew_table(base, span):
    groups = base.shape[0]
    padded = jnp.concatenate([base, jnp.zeros((groups, span + 1), jnp.float32)], axis=1)
    tiled = jnp.tile(padded[:, None, :], (1, span, 1)).reshape(groups, span * (2 * span + 1))
    return tiled[:, : span * 2 * span].reshape(groups, span, 2 * span)


def band_windows(extended, span, groups):
    chans = extended.shape[1]
    padded = jnp.concatenate([extended, jnp.zeros((1, chans), jnp.float32)], 0)
    blocks = padded.shape[0] // span
    padded = padded.reshape(blocks, span, groups, chans // groups)
    return jnp.concatenate([padded[:-1], padded[1:]], axis=1)


def band_apply(table, extended, span):
    groups = table.shape[0]
    chans = extended.shape[1]
    windows = band_windows(extended, span, groups).astype(jnp.bfloat16)
    high = table.astype(jnp.bfloat16)
    low = (table - high.astype(jnp.float32)).astype(jnp.bfloat16)
    result = jnp.einsum(
        "gtu,bugc->btgc", high, windows, preferred_element_type=jnp.float32
    ) + jnp.einsum("gtu,bugc->btgc", low, windows, preferred_element_type=jnp.float32)
    return result.reshape(windows.shape[0] * span, chans)


def band_grad(left, extended, span, groups):
    rows, chans = left.shape
    lhs = left.reshape(rows // span, span, groups, chans // groups)
    windows = band_windows(extended, span, groups).astype(jnp.bfloat16)
    prods = jnp.einsum(
        "btgc,bugc->gtu", lhs.astype(jnp.bfloat16), windows, preferred_element_type=jnp.float32
    )
    flat = jnp.concatenate(
        [prods.reshape(groups, span * 2 * span), jnp.zeros((groups, span), jnp.float32)], axis=1
    )
    skewed = flat.reshape(groups, span, 2 * span + 1).sum(axis=1)
    return jnp.flip(skewed[:, :span], axis=1).T


def short_apply(filters, extended, rows):
    taps = filters.shape[1]
    total = jnp.zeros((rows,) + extended.shape[1:], jnp.float32)
    for tap in range(taps):
        total = total + filters[:, tap][None] * extended[taps - 1 - tap : taps - 1 - tap + rows]
    return total


def per_device(activations, in_weight, out_weight, short_filter, mixer_filter, cotangent):
    rows_own = activations.shape[1]
    width = activations.shape[2]
    rows = rows_own * lax.axis_size("tchip") * lax.axis_size("core")
    span = mixer_filter.shape[0]
    groups = mixer_filter.shape[1]
    taps = short_filter.shape[1]
    chans = short_filter.shape[2]
    own = activations[0].astype(jnp.float32)
    inverse = lax.rsqrt(jnp.mean(own * own, axis=-1, keepdims=True) + EPS)
    normed = (own * inverse).astype(jnp.bfloat16)
    slab = lax.all_gather(normed, TENSOR, axis=0, tiled=True)
    full_in = pair_gather(in_weight, "dp", 0)
    full_out = pair_gather(out_weight, "dp", 1)
    in_flat = full_in.reshape(width, 3 * chans)
    projected = (
        jnp.dot(slab, in_flat, preferred_element_type=jnp.float32)
        .astype(jnp.bfloat16)
        .reshape(rows, 3, chans)
    )
    proj_wide = projected.astype(jnp.float32)
    table_fwd = skew_table(jnp.flip(mixer_filter, axis=0).T, span)
    table_back = skew_table(mixer_filter.T, span)
    short_rim = from_behind(projected[rows - taps + 1 :], "context", 1)
    proj_ext = jnp.concatenate([short_rim.astype(jnp.float32), proj_wide], 0)
    streams = short_apply(short_filter, proj_ext, rows)
    gated = (streams[:, 1] * streams[:, 2]).astype(jnp.bfloat16)
    gate_rim = from_behind(gated[rows - span + 1 :], "context", 1)
    gate_ext = jnp.concatenate([gate_rim, gated], 0).astype(jnp.float32)
    mixed = band_apply(table_fwd, gate_ext, span)
    output_rows = (streams[:, 0] * mixed).astype(jnp.bfloat16)
    piece = output_rows
    branch = pair_scatter_sum(
        jnp.dot(piece, full_out, preferred_element_type=jnp.float32).astype(jnp.bfloat16)
    )
    block_out = (own + branch).astype(jnp.bfloat16)[None]
    cot_slab = lax.all_gather(cotangent[0], TENSOR, axis=0, tiled=True)
    grad_rows = lax.dot_general(
        cot_slab, full_out, (((1,), (1,)), ((), ())), preferred_element_type=jnp.float32
    )
    out_term = lax.dot_general(
        output_rows, cot_slab, (((0,), (0,)), ((), ())), preferred_element_type=jnp.float32
    )
    grad_mix = (grad_rows * streams[:, 0]).astype(jnp.bfloat16)
    grad_mix_wide = grad_mix.astype(jnp.float32)
    mix_rim = from_behind(grad_mix[: span - 1], "context", -1)
    grad_gate = band_apply(
        table_back, jnp.concatenate([grad_mix_wide, mix_rim.astype(jnp.float32)], 0), span
    )
    mixer_term = band_grad(grad_mix_wide, gate_ext, span, groups)
    grad_streams = jnp.stack(
        [grad_rows * mixed, grad_gate * streams[:, 2], grad_gate * streams[:, 1]], axis=1
    )
    stream_rim = from_behind(grad_streams[: taps - 1], "context", -1)
    stream_ext = jnp.concatenate([grad_streams, stream_rim], 0)
    grad_proj = jnp.zeros((rows, 3, chans), jnp.float32)
    for tap in range(taps):
        grad_proj = grad_proj + short_filter[:, tap][None] * stream_ext[tap : tap + rows]
    grad_proj = grad_proj.astype(jnp.bfloat16)
    short_terms = [
        jnp.sum(grad_streams * proj_ext[taps - 1 - tap : taps - 1 - tap + rows], axis=0)
        for tap in range(taps)
    ]
    short_term = jnp.stack(short_terms, axis=1)
    flat = tree_psum(jnp.concatenate([short_term.ravel(), mixer_term.ravel()]), ("dp", "context"))
    grad_short = flat[: short_term.size].reshape(short_term.shape)
    grad_mixer = flat[short_term.size :].reshape(mixer_term.shape)
    proj_flat = grad_proj.reshape(rows, 3 * chans)
    in_term = lax.dot_general(
        slab, proj_flat, (((0,), (0,)), ((), ())), preferred_element_type=jnp.float32
    ).reshape(width, 3, chans)
    grad_in, grad_out = (
        lax.psum_scatter(
            in_term.astype(jnp.bfloat16), ("dp", "context"), scatter_dimension=0, tiled=True
        ).astype(jnp.float32),
        scatter_sum(out_term.astype(jnp.bfloat16), ("dp", "context"), 1),
    )
    piece = proj_flat
    grad_norm = pair_scatter_sum(
        lax.dot_general(
            piece, in_flat, (((1,), (1,)), ((), ())), preferred_element_type=jnp.float32
        ).astype(jnp.bfloat16)
    )
    grad_x = (
        cotangent[0].astype(jnp.float32)
        + inverse * grad_norm
        - own * inverse**3 * jnp.mean(grad_norm * own, axis=-1, keepdims=True)
    )
    grad_input = grad_x.astype(jnp.bfloat16)[None]
    return (
        block_out,
        grad_input,
        grad_in.astype(jnp.bfloat16),
        grad_out.astype(jnp.bfloat16),
        grad_short,
        grad_mixer,
    )


def solution(mesh):
    devices = mesh.devices
    lead = devices.shape[:2]
    cores = 2
    chips = devices.shape[2] // cores
    mesh = jax.sharding.Mesh(
        devices.reshape(lead + (chips, cores)), ("dp", "context", "tchip", "core")
    )
    placed = (
        P("dp", ("context", "tchip", "core"), None),
        P("dp", None, TENSOR),
        P(TENSOR, "dp"),
        P(None, None, TENSOR),
        P(None, TENSOR),
        P("dp", ("context", "tchip", "core"), None),
    )
    return jax.shard_map(
        per_device,
        mesh=mesh,
        in_specs=placed,
        out_specs=(
            P("dp", ("context", "tchip", "core"), None),
            P("dp", ("context", "tchip", "core"), None),
            P(("dp", "context"), None, TENSOR),
            P(TENSOR, ("dp", "context")),
            P(None, None, TENSOR),
            P(None, TENSOR),
        ),
        check_vma=False,
    )
```

```python
import jax
import jax.numpy as jnp
from jax import lax
from jax.sharding import PartitionSpec as P

EPS = 1e-05
TENSOR = ("tchip", "core")


def from_behind(value, axis, steps):
    count = lax.axis_size(axis)
    initial, last = (max(0, -steps), min(count, count - steps))
    return lax.ppermute(value, axis, [(source, source + steps) for source in range(initial, last)])


def pair_gather(value, axis, dim):
    count = lax.axis_size(axis)
    index = lax.axis_index(axis)
    parts = [value]
    for step in range(1, count):
        parts.append(lax.ppermute(value, axis, [(i, (i + step) % count) for i in range(count)]))
    shape = list(value.shape)
    size = shape[dim]
    shape[dim] = size * count
    full = jnp.zeros(shape, value.dtype)
    for step, part in enumerate(parts):
        start = [0] * len(shape)
        start[dim] = ((index - step) % count) * size
        full = lax.dynamic_update_slice(full, part, start)
    return full


def tree_psum(value, axes):
    for axis in axes:
        count = lax.axis_size(axis)
        if count & (count - 1):
            value = lax.psum(value, axis)
            continue
        step = 1
        while step < count:
            partner = lax.ppermute(value, axis, [(i, i ^ step) for i in range(count)])
            value = value + partner
            step *= 2
    return value


def pair_scatter_sum(value):
    chips = lax.axis_size("tchip")
    cores = lax.axis_size("core")
    rows, width = value.shape
    value = value.reshape(chips, cores, rows // (chips * cores), width)
    pieces = lax.all_to_all(value, "core", 1, 1)
    paired = jnp.sum(pieces.astype(jnp.float32), axis=1).astype(jnp.bfloat16)
    pieces = lax.all_to_all(paired, "tchip", 0, 0)
    return jnp.sum(pieces.astype(jnp.float32), axis=0)


def scatter_sum(value, axis, dim):
    count = lax.axis_size(axis)
    shape = value.shape
    split = shape[:dim] + (count, shape[dim] // count) + shape[dim + 1 :]
    pieces = lax.all_to_all(value.reshape(split), axis, dim, 0)
    return jnp.sum(pieces.astype(jnp.float32), axis=0)


def skew_table(base, span):
    groups = base.shape[0]
    padded = jnp.concatenate([base, jnp.zeros((groups, span + 1), jnp.float32)], axis=1)
    tiled = jnp.tile(padded[:, None, :], (1, span, 1)).reshape(groups, span * (2 * span + 1))
    return tiled[:, : span * 2 * span].reshape(groups, span, 2 * span)


def band_windows(extended, span, groups):
    chans = extended.shape[1]
    padded = jnp.concatenate([extended, jnp.zeros((1, chans), jnp.float32)], 0)
    blocks = padded.shape[0] // span
    padded = padded.reshape(blocks, span, groups, chans // groups)
    return jnp.concatenate([padded[:-1], padded[1:]], axis=1)


def band_apply(table, extended, span):
    groups = table.shape[0]
    chans = extended.shape[1]
    windows = band_windows(extended, span, groups).astype(jnp.bfloat16)
    high = table.astype(jnp.bfloat16)
    low = (table - high.astype(jnp.float32)).astype(jnp.bfloat16)
    result = jnp.einsum(
        "gtu,bugc->btgc", high, windows, preferred_element_type=jnp.float32
    ) + jnp.einsum("gtu,bugc->btgc", low, windows, preferred_element_type=jnp.float32)
    return result.reshape(windows.shape[0] * span, chans)


def band_grad(left, extended, span, groups):
    rows, chans = left.shape
    lhs = left.reshape(rows // span, span, groups, chans // groups)
    windows = band_windows(extended, span, groups).astype(jnp.bfloat16)
    prods = jnp.einsum(
        "btgc,bugc->gtu", lhs.astype(jnp.bfloat16), windows, preferred_element_type=jnp.float32
    )
    flat = jnp.concatenate(
        [prods.reshape(groups, span * 2 * span), jnp.zeros((groups, span), jnp.float32)], axis=1
    )
    skewed = flat.reshape(groups, span, 2 * span + 1).sum(axis=1)
    return jnp.flip(skewed[:, :span], axis=1).T


def short_apply(filters, extended, rows):
    taps = filters.shape[1]
    total = jnp.zeros((rows,) + extended.shape[1:], jnp.float32)
    for tap in range(taps):
        total = total + filters[:, tap][None] * extended[taps - 1 - tap : taps - 1 - tap + rows]
    return total


def per_device(activations, in_weight, out_weight, short_filter, mixer_filter, cotangent):
    rows_own = activations.shape[1]
    width = activations.shape[2]
    rows = rows_own * lax.axis_size("tchip") * lax.axis_size("core")
    span = mixer_filter.shape[0]
    groups = mixer_filter.shape[1]
    taps = short_filter.shape[1]
    chans = short_filter.shape[2]
    own = activations[0].astype(jnp.float32)
    inverse = lax.rsqrt(jnp.mean(own * own, axis=-1, keepdims=True) + EPS)
    normed = (own * inverse).astype(jnp.bfloat16)
    slab = lax.all_gather(normed, TENSOR, axis=0, tiled=True)
    full_in = pair_gather(in_weight, "dp", 0)
    full_out = pair_gather(out_weight, "dp", 1)
    in_flat = full_in.reshape(width, 3 * chans)
    projected = (
        jnp.dot(slab, in_flat, preferred_element_type=jnp.float32)
        .astype(jnp.bfloat16)
        .reshape(rows, 3, chans)
    )
    proj_wide = projected.astype(jnp.float32)
    table_fwd = skew_table(jnp.flip(mixer_filter, axis=0).T, span)
    table_back = skew_table(mixer_filter.T, span)
    short_rim = from_behind(projected[rows - taps + 1 :], "context", 1)
    proj_ext = jnp.concatenate([short_rim.astype(jnp.float32), proj_wide], 0)
    streams = short_apply(short_filter, proj_ext, rows)
    gated = (streams[:, 1] * streams[:, 2]).astype(jnp.bfloat16)
    gate_rim = from_behind(gated[rows - span + 1 :], "context", 1)
    gate_ext = jnp.concatenate([gate_rim, gated], 0).astype(jnp.float32)
    mixed = band_apply(table_fwd, gate_ext, span)
    output_rows = (streams[:, 0] * mixed).astype(jnp.bfloat16)
    piece = output_rows
    branch = pair_scatter_sum(
        jnp.dot(piece, full_out, preferred_element_type=jnp.float32).astype(jnp.bfloat16)
    )
    block_out = (own + branch).astype(jnp.bfloat16)[None]
    cot_slab = lax.all_gather(cotangent[0], TENSOR, axis=0, tiled=True)
    grad_rows = lax.dot_general(
        cot_slab, full_out, (((1,), (1,)), ((), ())), preferred_element_type=jnp.float32
    )
    out_term = lax.dot_general(
        cot_slab, output_rows, (((0,), (0,)), ((), ())), preferred_element_type=jnp.float32
    )
    grad_mix = (grad_rows * streams[:, 0]).astype(jnp.bfloat16)
    grad_mix_wide = grad_mix.astype(jnp.float32)
    mix_rim = from_behind(grad_mix[: span - 1], "context", -1)
    grad_gate = band_apply(
        table_back, jnp.concatenate([grad_mix_wide, mix_rim.astype(jnp.float32)], 0), span
    )
    mixer_term = band_grad(grad_mix_wide, gate_ext, span, groups)
    grad_streams = jnp.stack(
        [grad_rows * mixed, grad_gate * streams[:, 2], grad_gate * streams[:, 1]], axis=1
    )
    stream_rim = from_behind(grad_streams[: taps - 1], "context", -1)
    stream_ext = jnp.concatenate([grad_streams, stream_rim], 0)
    grad_proj = jnp.zeros((rows, 3, chans), jnp.float32)
    for tap in range(taps):
        grad_proj = grad_proj + short_filter[:, tap][None] * stream_ext[tap : tap + rows]
    grad_proj = grad_proj.astype(jnp.bfloat16)
    short_terms = [
        jnp.sum(grad_streams * proj_ext[taps - 1 - tap : taps - 1 - tap + rows], axis=0)
        for tap in range(taps)
    ]
    short_term = jnp.stack(short_terms, axis=1)
    flat = tree_psum(jnp.concatenate([short_term.ravel(), mixer_term.ravel()]), ("dp", "context"))
    grad_short = flat[: short_term.size].reshape(short_term.shape)
    grad_mixer = flat[short_term.size :].reshape(mixer_term.shape)
    proj_flat = grad_proj.reshape(rows, 3 * chans)
    in_term = lax.dot_general(
        slab, proj_flat, (((0,), (0,)), ((), ())), preferred_element_type=jnp.float32
    ).reshape(width, 3, chans)
    in_cols = in_term.shape[1] * in_term.shape[2]
    joined = jnp.concatenate(
        [in_term.reshape(width, in_cols).astype(jnp.bfloat16), out_term.astype(jnp.bfloat16)], 1
    )
    joined = lax.psum_scatter(joined, ("dp", "context"), scatter_dimension=0, tiled=True)
    grad_in = joined[:, :in_cols].reshape((-1,) + in_term.shape[1:])
    grad_out = joined[:, in_cols:].T
    piece = proj_flat
    grad_norm = pair_scatter_sum(
        lax.dot_general(
            piece, in_flat, (((1,), (1,)), ((), ())), preferred_element_type=jnp.float32
        ).astype(jnp.bfloat16)
    )
    grad_x = (
        cotangent[0].astype(jnp.float32)
        + inverse * grad_norm
        - own * inverse**3 * jnp.mean(grad_norm * own, axis=-1, keepdims=True)
    )
    grad_input = grad_x.astype(jnp.bfloat16)[None]
    return (
        block_out,
        grad_input,
        grad_in.astype(jnp.bfloat16),
        grad_out.astype(jnp.bfloat16),
        grad_short,
        grad_mixer,
    )


def solution(mesh):
    devices = mesh.devices
    lead = devices.shape[:2]
    cores = 2
    chips = devices.shape[2] // cores
    mesh = jax.sharding.Mesh(
        devices.reshape(lead + (chips, cores)), ("dp", "context", "tchip", "core")
    )
    placed = (
        P("dp", ("context", "tchip", "core"), None),
        P("dp", None, TENSOR),
        P(TENSOR, "dp"),
        P(None, None, TENSOR),
        P(None, TENSOR),
        P("dp", ("context", "tchip", "core"), None),
    )
    return jax.shard_map(
        per_device,
        mesh=mesh,
        in_specs=placed,
        out_specs=(
            P("dp", ("context", "tchip", "core"), None),
            P("dp", ("context", "tchip", "core"), None),
            P(("dp", "context"), None, TENSOR),
            P(TENSOR, ("dp", "context")),
            P(None, None, TENSOR),
            P(None, TENSOR),
        ),
        check_vma=False,
    )
```

```python
import jax
import jax.numpy as jnp
from jax import lax
from jax.sharding import PartitionSpec as P

EPS = 1e-05
TENSOR = ("tchip", "core")


def from_behind(value, axis, steps):
    count = lax.axis_size(axis)
    initial, last = (max(0, -steps), min(count, count - steps))
    return lax.ppermute(value, axis, [(source, source + steps) for source in range(initial, last)])


def pair_gather(value, axis, dim):
    count = lax.axis_size(axis)
    index = lax.axis_index(axis)
    parts = [value]
    for step in range(1, count):
        parts.append(lax.ppermute(value, axis, [(i, (i + step) % count) for i in range(count)]))
    shape = list(value.shape)
    size = shape[dim]
    shape[dim] = size * count
    full = jnp.zeros(shape, value.dtype)
    for step, part in enumerate(parts):
        start = [0] * len(shape)
        start[dim] = ((index - step) % count) * size
        full = lax.dynamic_update_slice(full, part, start)
    return full


def tree_psum(value, axes):
    for axis in axes:
        count = lax.axis_size(axis)
        if count & (count - 1):
            value = lax.psum(value, axis)
            continue
        step = 1
        while step < count:
            partner = lax.ppermute(value, axis, [(i, i ^ step) for i in range(count)])
            value = value + partner
            step *= 2
    return value


def pair_scatter_sum(value):
    chips = lax.axis_size("tchip")
    cores = lax.axis_size("core")
    rows, width = value.shape
    value = value.reshape(chips, cores, rows // (chips * cores), width)
    pieces = lax.all_to_all(value, "core", 1, 1)
    paired = jnp.sum(pieces.astype(jnp.float32), axis=1).astype(jnp.bfloat16)
    pieces = lax.all_to_all(paired, "tchip", 0, 0)
    return jnp.sum(pieces.astype(jnp.float32), axis=0)


def scatter_sum(value, axis, dim):
    count = lax.axis_size(axis)
    shape = value.shape
    split = shape[:dim] + (count, shape[dim] // count) + shape[dim + 1 :]
    pieces = lax.all_to_all(value.reshape(split), axis, dim, 0)
    return jnp.sum(pieces.astype(jnp.float32), axis=0)


def skew_table(base, span):
    groups = base.shape[0]
    padded = jnp.concatenate([base, jnp.zeros((groups, span + 1), jnp.float32)], axis=1)
    tiled = jnp.tile(padded[:, None, :], (1, span, 1)).reshape(groups, span * (2 * span + 1))
    return tiled[:, : span * 2 * span].reshape(groups, span, 2 * span)


def band_windows(extended, span, groups):
    chans = extended.shape[1]
    padded = jnp.concatenate([extended, jnp.zeros((1, chans), jnp.float32)], 0)
    blocks = padded.shape[0] // span
    padded = padded.reshape(blocks, span, groups, chans // groups)
    return jnp.concatenate([padded[:-1], padded[1:]], axis=1)


def band_apply(table, extended, span):
    groups = table.shape[0]
    chans = extended.shape[1]
    windows = band_windows(extended, span, groups).astype(jnp.bfloat16)
    high = table.astype(jnp.bfloat16)
    low = (table - high.astype(jnp.float32)).astype(jnp.bfloat16)
    result = jnp.einsum(
        "gtu,bugc->btgc", high, windows, preferred_element_type=jnp.float32
    ) + jnp.einsum("gtu,bugc->btgc", low, windows, preferred_element_type=jnp.float32)
    return result.reshape(windows.shape[0] * span, chans)


def band_grad(left, extended, span, groups):
    rows, chans = left.shape
    lhs = left.reshape(rows // span, span, groups, chans // groups)
    windows = band_windows(extended, span, groups).astype(jnp.bfloat16)
    prods = jnp.einsum(
        "btgc,bugc->gtu", lhs.astype(jnp.bfloat16), windows, preferred_element_type=jnp.float32
    )
    flat = jnp.concatenate(
        [prods.reshape(groups, span * 2 * span), jnp.zeros((groups, span), jnp.float32)], axis=1
    )
    skewed = flat.reshape(groups, span, 2 * span + 1).sum(axis=1)
    return jnp.flip(skewed[:, :span], axis=1).T


def short_apply(filters, extended, rows):
    taps = filters.shape[1]
    total = jnp.zeros((rows,) + extended.shape[1:], jnp.float32)
    for tap in range(taps):
        total = total + filters[:, tap][None] * extended[taps - 1 - tap : taps - 1 - tap + rows]
    return total


def per_device(activations, in_weight, out_weight, short_filter, mixer_filter, cotangent):
    rows_own = activations.shape[1]
    width = activations.shape[2]
    rows = rows_own * lax.axis_size("tchip") * lax.axis_size("core")
    span = mixer_filter.shape[0]
    groups = mixer_filter.shape[1]
    taps = short_filter.shape[1]
    chans = short_filter.shape[2]
    own = activations[0].astype(jnp.float32)
    inverse = lax.rsqrt(jnp.mean(own * own, axis=-1, keepdims=True) + EPS)
    normed = (own * inverse).astype(jnp.bfloat16)
    slab = lax.all_gather(normed, TENSOR, axis=0, tiled=True)
    full_in = pair_gather(in_weight, "dp", 0)
    full_out = pair_gather(out_weight, "dp", 1)
    in_flat = full_in.reshape(width, 3 * chans)
    projected = (
        jnp.dot(slab, in_flat, preferred_element_type=jnp.float32)
        .astype(jnp.bfloat16)
        .reshape(rows, 3, chans)
    )
    proj_wide = projected.astype(jnp.float32)
    table_fwd = skew_table(jnp.flip(mixer_filter, axis=0).T, span)
    table_back = skew_table(mixer_filter.T, span)
    short_rim = from_behind(projected[rows - taps + 1 :], "context", 1)
    proj_ext = jnp.concatenate([short_rim.astype(jnp.float32), proj_wide], 0)
    streams = short_apply(short_filter, proj_ext, rows)
    gated = (streams[:, 1] * streams[:, 2]).astype(jnp.bfloat16)
    gate_rim = from_behind(gated[rows - span + 1 :], "context", 1)
    gate_ext = jnp.concatenate([gate_rim, gated], 0).astype(jnp.float32)
    mixed = band_apply(table_fwd, gate_ext, span)
    output_rows = (streams[:, 0] * mixed).astype(jnp.bfloat16)
    piece = output_rows
    branch = pair_scatter_sum(
        jnp.dot(piece, full_out, preferred_element_type=jnp.float32).astype(jnp.bfloat16)
    )
    block_out = (own + branch).astype(jnp.bfloat16)[None]
    cot_slab = lax.all_gather(cotangent[0], TENSOR, axis=0, tiled=True)
    out_term = lax.dot_general(
        cot_slab, output_rows, (((0,), (0,)), ((), ())), preferred_element_type=jnp.float32
    ).astype(jnp.bfloat16)
    out_term, cot_slab = lax.optimization_barrier((out_term, cot_slab))
    grad_rows = lax.dot_general(
        cot_slab, full_out, (((1,), (1,)), ((), ())), preferred_element_type=jnp.float32
    )
    grad_mix = (grad_rows * streams[:, 0]).astype(jnp.bfloat16)
    grad_mix_wide = grad_mix.astype(jnp.float32)
    mix_rim = from_behind(grad_mix[: span - 1], "context", -1)
    grad_gate = band_apply(
        table_back, jnp.concatenate([grad_mix_wide, mix_rim.astype(jnp.float32)], 0), span
    )
    mixer_term = band_grad(grad_mix_wide, gate_ext, span, groups)
    grad_streams = jnp.stack(
        [grad_rows * mixed, grad_gate * streams[:, 2], grad_gate * streams[:, 1]], axis=1
    )
    stream_rim = from_behind(grad_streams[: taps - 1], "context", -1)
    stream_ext = jnp.concatenate([grad_streams, stream_rim], 0)
    grad_proj = jnp.zeros((rows, 3, chans), jnp.float32)
    for tap in range(taps):
        grad_proj = grad_proj + short_filter[:, tap][None] * stream_ext[tap : tap + rows]
    grad_proj = grad_proj.astype(jnp.bfloat16)
    short_terms = [
        jnp.sum(grad_streams * proj_ext[taps - 1 - tap : taps - 1 - tap + rows], axis=0)
        for tap in range(taps)
    ]
    short_term = jnp.stack(short_terms, axis=1)
    flat = tree_psum(jnp.concatenate([short_term.ravel(), mixer_term.ravel()]), ("dp", "context"))
    grad_short = flat[: short_term.size].reshape(short_term.shape)
    grad_mixer = flat[short_term.size :].reshape(mixer_term.shape)
    proj_flat = grad_proj.reshape(rows, 3 * chans)
    in_term = lax.dot_general(
        slab, proj_flat, (((0,), (0,)), ((), ())), preferred_element_type=jnp.float32
    ).reshape(width, 3, chans)
    grad_in, grad_out = (
        lax.psum_scatter(
            in_term.astype(jnp.bfloat16), ("dp", "context"), scatter_dimension=0, tiled=True
        ).astype(jnp.float32),
        lax.psum_scatter(out_term, ("dp", "context"), scatter_dimension=0, tiled=True).T,
    )
    piece = proj_flat
    grad_norm = pair_scatter_sum(
        lax.dot_general(
            piece, in_flat, (((1,), (1,)), ((), ())), preferred_element_type=jnp.float32
        ).astype(jnp.bfloat16)
    )
    grad_x = (
        cotangent[0].astype(jnp.float32)
        + inverse * grad_norm
        - own * inverse**3 * jnp.mean(grad_norm * own, axis=-1, keepdims=True)
    )
    grad_input = grad_x.astype(jnp.bfloat16)[None]
    return (
        block_out,
        grad_input,
        grad_in.astype(jnp.bfloat16),
        grad_out.astype(jnp.bfloat16),
        grad_short,
        grad_mixer,
    )


def solution(mesh):
    devices = mesh.devices
    lead = devices.shape[:2]
    cores = 2
    chips = devices.shape[2] // cores
    mesh = jax.sharding.Mesh(
        devices.reshape(lead + (chips, cores)), ("dp", "context", "tchip", "core")
    )
    placed = (
        P("dp", ("context", "tchip", "core"), None),
        P("dp", None, TENSOR),
        P(TENSOR, "dp"),
        P(None, None, TENSOR),
        P(None, TENSOR),
        P("dp", ("context", "tchip", "core"), None),
    )
    return jax.shard_map(
        per_device,
        mesh=mesh,
        in_specs=placed,
        out_specs=(
            P("dp", ("context", "tchip", "core"), None),
            P("dp", ("context", "tchip", "core"), None),
            P(("dp", "context"), None, TENSOR),
            P(TENSOR, ("dp", "context")),
            P(None, None, TENSOR),
            P(None, TENSOR),
        ),
        check_vma=False,
    )
```

```python
import jax
import jax.numpy as jnp
from jax import lax
from jax.sharding import PartitionSpec as P

EPS = 1e-05
TENSOR = ("tchip", "core")


def from_behind(value, axis, steps):
    count = lax.axis_size(axis)
    initial, last = (max(0, -steps), min(count, count - steps))
    return lax.ppermute(value, axis, [(source, source + steps) for source in range(initial, last)])


def pair_gather(value, axis, dim):
    count = lax.axis_size(axis)
    index = lax.axis_index(axis)
    parts = [value]
    for step in range(1, count):
        parts.append(lax.ppermute(value, axis, [(i, (i + step) % count) for i in range(count)]))
    shape = list(value.shape)
    size = shape[dim]
    shape[dim] = size * count
    full = jnp.zeros(shape, value.dtype)
    for step, part in enumerate(parts):
        start = [0] * len(shape)
        start[dim] = ((index - step) % count) * size
        full = lax.dynamic_update_slice(full, part, start)
    return full


def tree_psum(value, axes):
    for axis in axes:
        count = lax.axis_size(axis)
        if count & (count - 1):
            value = lax.psum(value, axis)
            continue
        step = 1
        while step < count:
            partner = lax.ppermute(value, axis, [(i, i ^ step) for i in range(count)])
            value = value + partner
            step *= 2
    return value


def pair_scatter_sum(value):
    chips = lax.axis_size("tchip")
    cores = lax.axis_size("core")
    rows, width = value.shape
    value = value.reshape(chips, cores, rows // (chips * cores), width)
    pieces = lax.all_to_all(value, "core", 1, 1)
    paired = jnp.sum(pieces.astype(jnp.float32), axis=1).astype(jnp.bfloat16)
    pieces = lax.all_to_all(paired, "tchip", 0, 0)
    return jnp.sum(pieces.astype(jnp.float32), axis=0)


def scatter_sum(value, axis, dim):
    count = lax.axis_size(axis)
    shape = value.shape
    split = shape[:dim] + (count, shape[dim] // count) + shape[dim + 1 :]
    pieces = lax.all_to_all(value.reshape(split), axis, dim, 0)
    return jnp.sum(pieces.astype(jnp.float32), axis=0)


def skew_table(base, span):
    groups = base.shape[0]
    padded = jnp.concatenate([base, jnp.zeros((groups, span + 1), jnp.float32)], axis=1)
    tiled = jnp.tile(padded[:, None, :], (1, span, 1)).reshape(groups, span * (2 * span + 1))
    return tiled[:, : span * 2 * span].reshape(groups, span, 2 * span)


def band_windows(extended, span, groups):
    chans = extended.shape[1]
    padded = jnp.concatenate([extended, jnp.zeros((1, chans), jnp.float32)], 0)
    blocks = padded.shape[0] // span
    padded = padded.reshape(blocks, span, groups, chans // groups)
    return jnp.concatenate([padded[:-1], padded[1:]], axis=1)


def band_apply(table, extended, span):
    groups = table.shape[0]
    chans = extended.shape[1]
    windows = band_windows(extended, span, groups).astype(jnp.bfloat16)
    high = table.astype(jnp.bfloat16)
    low = (table - high.astype(jnp.float32)).astype(jnp.bfloat16)
    result = jnp.einsum(
        "gtu,bugc->btgc", high, windows, preferred_element_type=jnp.float32
    ) + jnp.einsum("gtu,bugc->btgc", low, windows, preferred_element_type=jnp.float32)
    return result.reshape(windows.shape[0] * span, chans)


def band_grad(left, extended, span, groups):
    rows, chans = left.shape
    lhs = left.reshape(rows // span, span, groups, chans // groups)
    windows = band_windows(extended, span, groups).astype(jnp.bfloat16)
    prods = jnp.einsum(
        "btgc,bugc->gtu", lhs.astype(jnp.bfloat16), windows, preferred_element_type=jnp.float32
    )
    flat = jnp.concatenate(
        [prods.reshape(groups, span * 2 * span), jnp.zeros((groups, span), jnp.float32)], axis=1
    )
    skewed = flat.reshape(groups, span, 2 * span + 1).sum(axis=1)
    return jnp.flip(skewed[:, :span], axis=1).T


def short_apply(filters, extended, rows):
    taps = filters.shape[1]
    total = jnp.zeros((rows,) + extended.shape[1:], jnp.float32)
    for tap in range(taps):
        total = total + filters[:, tap][None] * extended[taps - 1 - tap : taps - 1 - tap + rows]
    return total


def per_device(activations, in_weight, out_weight, short_filter, mixer_filter, cotangent):
    rows_own = activations.shape[1]
    width = activations.shape[2]
    rows = rows_own * lax.axis_size("tchip") * lax.axis_size("core")
    span = mixer_filter.shape[0]
    groups = mixer_filter.shape[1]
    taps = short_filter.shape[1]
    chans = short_filter.shape[2]
    own = activations[0].astype(jnp.float32)
    inverse = lax.rsqrt(jnp.mean(own * own, axis=-1, keepdims=True) + EPS)
    normed = (own * inverse).astype(jnp.bfloat16)
    slab = lax.all_gather(normed, TENSOR, axis=0, tiled=True)
    full_in = pair_gather(in_weight, "dp", 0)
    full_out = pair_gather(out_weight, "dp", 1)
    in_flat = full_in.reshape(width, 3 * chans)
    projected = (
        jnp.dot(slab, in_flat, preferred_element_type=jnp.float32)
        .astype(jnp.bfloat16)
        .reshape(rows, 3, chans)
    )
    proj_wide = projected.astype(jnp.float32)
    table_fwd = skew_table(jnp.flip(mixer_filter, axis=0).T, span)
    table_back = skew_table(mixer_filter.T, span)
    short_rim = from_behind(projected[rows - taps + 1 :], "context", 1)
    proj_ext = jnp.concatenate([short_rim.astype(jnp.float32), proj_wide], 0)
    streams = short_apply(short_filter, proj_ext, rows)
    gated = (streams[:, 1] * streams[:, 2]).astype(jnp.bfloat16)
    gate_rim = from_behind(gated[rows - span + 1 :], "context", 1)
    gate_ext = jnp.concatenate([gate_rim, gated], 0).astype(jnp.float32)
    mixed = band_apply(table_fwd, gate_ext, span)
    output_rows = (streams[:, 0] * mixed).astype(jnp.bfloat16)
    piece = output_rows
    branch = pair_scatter_sum(
        jnp.dot(piece, full_out, preferred_element_type=jnp.float32).astype(jnp.bfloat16)
    )
    cot_slab = lax.all_gather(cotangent[0], TENSOR, axis=0, tiled=True)
    out_term = lax.dot_general(
        cot_slab, output_rows, (((0,), (0,)), ((), ())), preferred_element_type=jnp.float32
    ).astype(jnp.bfloat16)
    out_term, cot_slab = lax.optimization_barrier((out_term, cot_slab))
    grad_rows = lax.dot_general(
        cot_slab, full_out, (((1,), (1,)), ((), ())), preferred_element_type=jnp.float32
    )
    grad_mix = (grad_rows * streams[:, 0]).astype(jnp.bfloat16)
    grad_mix_wide = grad_mix.astype(jnp.float32)
    mix_rim = from_behind(grad_mix[: span - 1], "context", -1)
    grad_gate = band_apply(
        table_back, jnp.concatenate([grad_mix_wide, mix_rim.astype(jnp.float32)], 0), span
    )
    mixer_term = band_grad(grad_mix_wide, gate_ext, span, groups)
    grad_streams = jnp.stack(
        [grad_rows * mixed, grad_gate * streams[:, 2], grad_gate * streams[:, 1]], axis=1
    )
    branch, grad_streams = lax.optimization_barrier((branch, grad_streams))
    block_out = (own + branch).astype(jnp.bfloat16)[None]
    stream_rim = from_behind(grad_streams[: taps - 1], "context", -1)
    stream_ext = jnp.concatenate([grad_streams, stream_rim], 0)
    grad_proj = jnp.zeros((rows, 3, chans), jnp.float32)
    for tap in range(taps):
        grad_proj = grad_proj + short_filter[:, tap][None] * stream_ext[tap : tap + rows]
    grad_proj = grad_proj.astype(jnp.bfloat16)
    short_terms = [
        jnp.sum(grad_streams * proj_ext[taps - 1 - tap : taps - 1 - tap + rows], axis=0)
        for tap in range(taps)
    ]
    short_term = jnp.stack(short_terms, axis=1)
    filters = tree_psum(
        jnp.concatenate([short_term.ravel(), mixer_term.ravel()]), ("dp", "context")
    )
    proj_flat = grad_proj.reshape(rows, 3 * chans)
    in_term = lax.dot_general(
        slab, proj_flat, (((0,), (0,)), ((), ())), preferred_element_type=jnp.float32
    ).reshape(width, 3, chans)
    grad_in, grad_out = (
        lax.psum_scatter(
            in_term.astype(jnp.bfloat16), ("dp", "context"), scatter_dimension=0, tiled=True
        ).astype(jnp.float32),
        lax.psum_scatter(out_term, ("dp", "context"), scatter_dimension=0, tiled=True).T,
    )
    piece = proj_flat
    norm_part = lax.dot_general(
        piece, in_flat, (((1,), (1,)), ((), ())), preferred_element_type=jnp.float32
    ).astype(jnp.bfloat16)
    filters, norm_part = lax.optimization_barrier((filters, norm_part))
    grad_short = filters[: short_term.size].reshape(short_term.shape)
    grad_mixer = filters[short_term.size :].reshape(mixer_term.shape)
    grad_norm = pair_scatter_sum(norm_part)
    grad_x = (
        cotangent[0].astype(jnp.float32)
        + inverse * grad_norm
        - own * inverse**3 * jnp.mean(grad_norm * own, axis=-1, keepdims=True)
    )
    grad_input = grad_x.astype(jnp.bfloat16)[None]
    return (
        block_out,
        grad_input,
        grad_in.astype(jnp.bfloat16),
        grad_out.astype(jnp.bfloat16),
        grad_short,
        grad_mixer,
    )


def solution(mesh):
    devices = mesh.devices
    lead = devices.shape[:2]
    cores = 2
    chips = devices.shape[2] // cores
    mesh = jax.sharding.Mesh(
        devices.reshape(lead + (chips, cores)), ("dp", "context", "tchip", "core")
    )
    placed = (
        P("dp", ("context", "tchip", "core"), None),
        P("dp", None, TENSOR),
        P(TENSOR, "dp"),
        P(None, None, TENSOR),
        P(None, TENSOR),
        P("dp", ("context", "tchip", "core"), None),
    )
    return jax.shard_map(
        per_device,
        mesh=mesh,
        in_specs=placed,
        out_specs=(
            P("dp", ("context", "tchip", "core"), None),
            P("dp", ("context", "tchip", "core"), None),
            P(("dp", "context"), None, TENSOR),
            P(TENSOR, ("dp", "context")),
            P(None, None, TENSOR),
            P(None, TENSOR),
        ),
        check_vma=False,
    )
```

```python
import jax
import jax.numpy as jnp
from jax import lax
from jax.sharding import PartitionSpec as P

EPS = 1e-05
TENSOR = ("tchip", "core")


def from_behind(value, axis, steps):
    count = lax.axis_size(axis)
    initial, last = (max(0, -steps), min(count, count - steps))
    return lax.ppermute(value, axis, [(source, source + steps) for source in range(initial, last)])


def pair_gather(value, axis, dim):
    count = lax.axis_size(axis)
    index = lax.axis_index(axis)
    parts = [value]
    for step in range(1, count):
        parts.append(lax.ppermute(value, axis, [(i, (i + step) % count) for i in range(count)]))
    shape = list(value.shape)
    size = shape[dim]
    shape[dim] = size * count
    full = jnp.zeros(shape, value.dtype)
    for step, part in enumerate(parts):
        start = [0] * len(shape)
        start[dim] = ((index - step) % count) * size
        full = lax.dynamic_update_slice(full, part, start)
    return full


def tree_psum(value, axes):
    for axis in axes:
        count = lax.axis_size(axis)
        if count & (count - 1):
            value = lax.psum(value, axis)
            continue
        step = 1
        while step < count:
            partner = lax.ppermute(value, axis, [(i, i ^ step) for i in range(count)])
            value = value + partner
            step *= 2
    return value


def pair_scatter_sum(value):
    chips = lax.axis_size("tchip")
    cores = lax.axis_size("core")
    rows, width = value.shape
    value = value.reshape(chips, cores, rows // (chips * cores), width)
    pieces = lax.all_to_all(value, "core", 1, 1)
    paired = jnp.sum(pieces.astype(jnp.float32), axis=1).astype(jnp.bfloat16)
    pieces = lax.all_to_all(paired, "tchip", 0, 0)
    return jnp.sum(pieces.astype(jnp.float32), axis=0)


def scatter_sum(value, axis, dim):
    count = lax.axis_size(axis)
    shape = value.shape
    split = shape[:dim] + (count, shape[dim] // count) + shape[dim + 1 :]
    pieces = lax.all_to_all(value.reshape(split), axis, dim, 0)
    return jnp.sum(pieces.astype(jnp.float32), axis=0)


def skew_table(base, span):
    groups = base.shape[0]
    padded = jnp.concatenate([base, jnp.zeros((groups, span + 1), jnp.float32)], axis=1)
    tiled = jnp.tile(padded[:, None, :], (1, span, 1)).reshape(groups, span * (2 * span + 1))
    return tiled[:, : span * 2 * span].reshape(groups, span, 2 * span)


def band_windows(extended, span, groups):
    chans = extended.shape[1]
    padded = jnp.concatenate([extended, jnp.zeros((1, chans), jnp.float32)], 0)
    blocks = padded.shape[0] // span
    padded = padded.reshape(blocks, span, groups, chans // groups)
    return jnp.concatenate([padded[:-1], padded[1:]], axis=1)


def band_apply(table, extended, span):
    groups = table.shape[0]
    chans = extended.shape[1]
    windows = band_windows(extended, span, groups).astype(jnp.bfloat16)
    high = table.astype(jnp.bfloat16)
    low = (table - high.astype(jnp.float32)).astype(jnp.bfloat16)
    result = jnp.einsum(
        "gtu,bugc->btgc", high, windows, preferred_element_type=jnp.float32
    ) + jnp.einsum("gtu,bugc->btgc", low, windows, preferred_element_type=jnp.float32)
    return result.reshape(windows.shape[0] * span, chans)


def band_grad(left, extended, span, groups):
    rows, chans = left.shape
    lhs = left.reshape(rows // span, span, groups, chans // groups)
    windows = band_windows(extended, span, groups).astype(jnp.bfloat16)
    prods = jnp.einsum(
        "btgc,bugc->gtu", lhs.astype(jnp.bfloat16), windows, preferred_element_type=jnp.float32
    )
    flat = jnp.concatenate(
        [prods.reshape(groups, span * 2 * span), jnp.zeros((groups, span), jnp.float32)], axis=1
    )
    skewed = flat.reshape(groups, span, 2 * span + 1).sum(axis=1)
    return jnp.flip(skewed[:, :span], axis=1).T


def short_apply(filters, extended, rows):
    taps = filters.shape[1]
    total = jnp.zeros((rows,) + extended.shape[1:], jnp.float32)
    for tap in range(taps):
        total = total + filters[:, tap][None] * extended[taps - 1 - tap : taps - 1 - tap + rows]
    return total


def per_device(activations, in_weight, out_weight, short_filter, mixer_filter, cotangent):
    rows_own = activations.shape[1]
    width = activations.shape[2]
    rows = rows_own * lax.axis_size("tchip") * lax.axis_size("core")
    span = mixer_filter.shape[0]
    groups = mixer_filter.shape[1]
    taps = short_filter.shape[1]
    chans = short_filter.shape[2]
    own = activations[0].astype(jnp.float32)
    inverse = lax.rsqrt(jnp.mean(own * own, axis=-1, keepdims=True) + EPS)
    normed = (own * inverse).astype(jnp.bfloat16)
    slab = lax.all_gather(normed, TENSOR, axis=0, tiled=True)
    full_in = pair_gather(in_weight, "dp", 0)
    full_in, out_weight = lax.optimization_barrier((full_in, out_weight))
    full_out = pair_gather(out_weight, "dp", 1)
    in_flat = full_in.reshape(width, 3 * chans)
    projected = (
        jnp.dot(slab, in_flat, preferred_element_type=jnp.float32)
        .astype(jnp.bfloat16)
        .reshape(rows, 3, chans)
    )
    proj_wide = projected.astype(jnp.float32)
    table_fwd = skew_table(jnp.flip(mixer_filter, axis=0).T, span)
    table_back = skew_table(mixer_filter.T, span)
    short_rim = from_behind(projected[rows - taps + 1 :], "context", 1)
    proj_ext = jnp.concatenate([short_rim.astype(jnp.float32), proj_wide], 0)
    streams = short_apply(short_filter, proj_ext, rows)
    gated = (streams[:, 1] * streams[:, 2]).astype(jnp.bfloat16)
    gate_rim = from_behind(gated[rows - span + 1 :], "context", 1)
    gate_ext = jnp.concatenate([gate_rim, gated], 0).astype(jnp.float32)
    mixed = band_apply(table_fwd, gate_ext, span)
    output_rows = (streams[:, 0] * mixed).astype(jnp.bfloat16)
    piece = output_rows
    branch = pair_scatter_sum(
        jnp.dot(piece, full_out, preferred_element_type=jnp.float32).astype(jnp.bfloat16)
    )
    cot_slab = lax.all_gather(cotangent[0], TENSOR, axis=0, tiled=True)
    out_term = lax.dot_general(
        cot_slab, output_rows, (((0,), (0,)), ((), ())), preferred_element_type=jnp.float32
    ).astype(jnp.bfloat16)
    out_term, cot_slab = lax.optimization_barrier((out_term, cot_slab))
    grad_rows = lax.dot_general(
        cot_slab, full_out, (((1,), (1,)), ((), ())), preferred_element_type=jnp.float32
    )
    grad_mix = (grad_rows * streams[:, 0]).astype(jnp.bfloat16)
    grad_mix_wide = grad_mix.astype(jnp.float32)
    mix_rim = from_behind(grad_mix[: span - 1], "context", -1)
    grad_gate = band_apply(
        table_back, jnp.concatenate([grad_mix_wide, mix_rim.astype(jnp.float32)], 0), span
    )
    mixer_term = band_grad(grad_mix_wide, gate_ext, span, groups)
    grad_streams = jnp.stack(
        [grad_rows * mixed, grad_gate * streams[:, 2], grad_gate * streams[:, 1]], axis=1
    )
    branch, grad_streams = lax.optimization_barrier((branch, grad_streams))
    block_out = (own + branch).astype(jnp.bfloat16)[None]
    stream_rim = from_behind(grad_streams[: taps - 1], "context", -1)
    stream_ext = jnp.concatenate([grad_streams, stream_rim], 0)
    grad_proj = jnp.zeros((rows, 3, chans), jnp.float32)
    for tap in range(taps):
        grad_proj = grad_proj + short_filter[:, tap][None] * stream_ext[tap : tap + rows]
    grad_proj = grad_proj.astype(jnp.bfloat16)
    short_terms = [
        jnp.sum(grad_streams * proj_ext[taps - 1 - tap : taps - 1 - tap + rows], axis=0)
        for tap in range(taps)
    ]
    short_term = jnp.stack(short_terms, axis=1)
    filters = tree_psum(
        jnp.concatenate([short_term.ravel(), mixer_term.ravel()]), ("dp", "context")
    )
    proj_flat = grad_proj.reshape(rows, 3 * chans)
    in_term = lax.dot_general(
        slab, proj_flat, (((0,), (0,)), ((), ())), preferred_element_type=jnp.float32
    ).reshape(width, 3, chans)
    grad_in, grad_out = (
        lax.psum_scatter(
            in_term.astype(jnp.bfloat16), ("dp", "context"), scatter_dimension=0, tiled=True
        ).astype(jnp.float32),
        lax.psum_scatter(out_term, ("dp", "context"), scatter_dimension=0, tiled=True).T,
    )
    piece = proj_flat
    norm_part = lax.dot_general(
        piece, in_flat, (((1,), (1,)), ((), ())), preferred_element_type=jnp.float32
    ).astype(jnp.bfloat16)
    filters, norm_part = lax.optimization_barrier((filters, norm_part))
    grad_short = filters[: short_term.size].reshape(short_term.shape)
    grad_mixer = filters[short_term.size :].reshape(mixer_term.shape)
    grad_norm = pair_scatter_sum(norm_part)
    grad_x = (
        cotangent[0].astype(jnp.float32)
        + inverse * grad_norm
        - own * inverse**3 * jnp.mean(grad_norm * own, axis=-1, keepdims=True)
    )
    grad_input = grad_x.astype(jnp.bfloat16)[None]
    return (
        block_out,
        grad_input,
        grad_in.astype(jnp.bfloat16),
        grad_out.astype(jnp.bfloat16),
        grad_short,
        grad_mixer,
    )


def solution(mesh):
    devices = mesh.devices
    lead = devices.shape[:2]
    cores = 2
    chips = devices.shape[2] // cores
    mesh = jax.sharding.Mesh(
        devices.reshape(lead + (chips, cores)), ("dp", "context", "tchip", "core")
    )
    placed = (
        P("dp", ("context", "tchip", "core"), None),
        P("dp", None, TENSOR),
        P(TENSOR, "dp"),
        P(None, None, TENSOR),
        P(None, TENSOR),
        P("dp", ("context", "tchip", "core"), None),
    )
    return jax.shard_map(
        per_device,
        mesh=mesh,
        in_specs=placed,
        out_specs=(
            P("dp", ("context", "tchip", "core"), None),
            P("dp", ("context", "tchip", "core"), None),
            P(("dp", "context"), None, TENSOR),
            P(TENSOR, ("dp", "context")),
            P(None, None, TENSOR),
            P(None, TENSOR),
        ),
        check_vma=False,
    )
```

```python
import jax
import jax.numpy as jnp
from jax import lax
from jax.sharding import PartitionSpec as P

EPS = 1e-05
TENSOR = ("tchip", "core")


def from_behind(value, axis, steps):
    count = lax.axis_size(axis)
    initial, last = (max(0, -steps), min(count, count - steps))
    return lax.ppermute(value, axis, [(source, source + steps) for source in range(initial, last)])


def pair_gather(value, axis, dim):
    count = lax.axis_size(axis)
    index = lax.axis_index(axis)
    parts = [value]
    for step in range(1, count):
        parts.append(lax.ppermute(value, axis, [(i, (i + step) % count) for i in range(count)]))
    shape = list(value.shape)
    size = shape[dim]
    shape[dim] = size * count
    full = jnp.zeros(shape, value.dtype)
    for step, part in enumerate(parts):
        start = [0] * len(shape)
        start[dim] = ((index - step) % count) * size
        full = lax.dynamic_update_slice(full, part, start)
    return full


def tree_psum(value, axes):
    for axis in axes:
        count = lax.axis_size(axis)
        if count & (count - 1):
            value = lax.psum(value, axis)
            continue
        step = 1
        while step < count:
            partner = lax.ppermute(value, axis, [(i, i ^ step) for i in range(count)])
            value = value + partner
            step *= 2
    return value


def pair_scatter_sum(value):
    chips = lax.axis_size("tchip")
    cores = lax.axis_size("core")
    rows, width = value.shape
    value = value.reshape(chips, cores, rows // (chips * cores), width)
    pieces = lax.all_to_all(value, "core", 1, 1)
    paired = jnp.sum(pieces.astype(jnp.float32), axis=1).astype(jnp.bfloat16)
    pieces = lax.all_to_all(paired, "tchip", 0, 0)
    return jnp.sum(pieces.astype(jnp.float32), axis=0)


def scatter_sum(value, axis, dim):
    count = lax.axis_size(axis)
    shape = value.shape
    split = shape[:dim] + (count, shape[dim] // count) + shape[dim + 1 :]
    pieces = lax.all_to_all(value.reshape(split), axis, dim, 0)
    return jnp.sum(pieces.astype(jnp.float32), axis=0)


def skew_table(base, span):
    groups = base.shape[0]
    padded = jnp.concatenate([base, jnp.zeros((groups, span + 1), jnp.float32)], axis=1)
    tiled = jnp.tile(padded[:, None, :], (1, span, 1)).reshape(groups, span * (2 * span + 1))
    return tiled[:, : span * 2 * span].reshape(groups, span, 2 * span)


def band_windows(extended, span, groups):
    chans = extended.shape[1]
    padded = jnp.concatenate([extended, jnp.zeros((1, chans), jnp.float32)], 0)
    blocks = padded.shape[0] // span
    padded = padded.reshape(blocks, span, groups, chans // groups)
    return jnp.concatenate([padded[:-1], padded[1:]], axis=1)


def band_apply(table, extended, span):
    groups = table.shape[0]
    chans = extended.shape[1]
    windows = band_windows(extended, span, groups).astype(jnp.bfloat16)
    high = table.astype(jnp.bfloat16)
    low = (table - high.astype(jnp.float32)).astype(jnp.bfloat16)
    result = jnp.einsum(
        "gtu,bugc->btgc", high, windows, preferred_element_type=jnp.float32
    ) + jnp.einsum("gtu,bugc->btgc", low, windows, preferred_element_type=jnp.float32)
    return result.reshape(windows.shape[0] * span, chans)


def band_grad(left, extended, span, groups):
    rows, chans = left.shape
    lhs = left.reshape(rows // span, span, groups, chans // groups)
    windows = band_windows(extended, span, groups).astype(jnp.bfloat16)
    prods = jnp.einsum(
        "btgc,bugc->gtu", lhs.astype(jnp.bfloat16), windows, preferred_element_type=jnp.float32
    )
    flat = jnp.concatenate(
        [prods.reshape(groups, span * 2 * span), jnp.zeros((groups, span), jnp.float32)], axis=1
    )
    skewed = flat.reshape(groups, span, 2 * span + 1).sum(axis=1)
    return jnp.flip(skewed[:, :span], axis=1).T


def short_apply(filters, extended, rows):
    taps = filters.shape[1]
    total = jnp.zeros((rows,) + extended.shape[1:], jnp.float32)
    for tap in range(taps):
        total = total + filters[:, tap][None] * extended[taps - 1 - tap : taps - 1 - tap + rows]
    return total


def per_device(activations, in_weight, out_weight, short_filter, mixer_filter, cotangent):
    rows_own = activations.shape[1]
    width = activations.shape[2]
    rows = rows_own * lax.axis_size("tchip") * lax.axis_size("core")
    span = mixer_filter.shape[0]
    groups = mixer_filter.shape[1]
    taps = short_filter.shape[1]
    chans = short_filter.shape[2]
    own = activations[0].astype(jnp.float32)
    inverse = lax.rsqrt(jnp.mean(own * own, axis=-1, keepdims=True) + EPS)
    normed = (own * inverse).astype(jnp.bfloat16)
    slab = lax.all_gather(normed, TENSOR, axis=0, tiled=True)
    full_in = pair_gather(in_weight, "dp", 0)
    full_out = pair_gather(out_weight, "dp", 1)
    in_flat = full_in.reshape(width, 3 * chans)
    projected = (
        jnp.dot(slab, in_flat, preferred_element_type=jnp.float32)
        .astype(jnp.bfloat16)
        .reshape(rows, 3, chans)
    )
    proj_wide = projected.astype(jnp.float32)
    table_fwd = skew_table(jnp.flip(mixer_filter, axis=0).T, span)
    table_back = skew_table(mixer_filter.T, span)
    wide_rim = from_behind(projected[rows - span - taps + 2 :], "context", 1)
    short_rim = wide_rim[span - 1 :]
    proj_ext = jnp.concatenate([short_rim.astype(jnp.float32), proj_wide], 0)
    streams = short_apply(short_filter, proj_ext, rows)
    gated = (streams[:, 1] * streams[:, 2]).astype(jnp.bfloat16)
    rim_streams = short_apply(short_filter, wide_rim.astype(jnp.float32), span - 1)
    gate_rim = (rim_streams[:, 1] * rim_streams[:, 2]).astype(jnp.bfloat16)
    gate_ext = jnp.concatenate([gate_rim, gated], 0).astype(jnp.float32)
    mixed = band_apply(table_fwd, gate_ext, span)
    output_rows = (streams[:, 0] * mixed).astype(jnp.bfloat16)
    piece = output_rows
    branch = pair_scatter_sum(
        jnp.dot(piece, full_out, preferred_element_type=jnp.float32).astype(jnp.bfloat16)
    )
    cot_slab = lax.all_gather(cotangent[0], TENSOR, axis=0, tiled=True)
    out_term = lax.dot_general(
        cot_slab, output_rows, (((0,), (0,)), ((), ())), preferred_element_type=jnp.float32
    ).astype(jnp.bfloat16)
    out_term, cot_slab = lax.optimization_barrier((out_term, cot_slab))
    grad_rows = lax.dot_general(
        cot_slab, full_out, (((1,), (1,)), ((), ())), preferred_element_type=jnp.float32
    )
    grad_mix = (grad_rows * streams[:, 0]).astype(jnp.bfloat16)
    grad_mix_wide = grad_mix.astype(jnp.float32)
    mix_rim = from_behind(grad_mix[: span - 1], "context", -1)
    grad_gate = band_apply(
        table_back, jnp.concatenate([grad_mix_wide, mix_rim.astype(jnp.float32)], 0), span
    )
    mixer_term = band_grad(grad_mix_wide, gate_ext, span, groups)
    grad_streams = jnp.stack(
        [grad_rows * mixed, grad_gate * streams[:, 2], grad_gate * streams[:, 1]], axis=1
    )
    branch, grad_streams = lax.optimization_barrier((branch, grad_streams))
    block_out = (own + branch).astype(jnp.bfloat16)[None]
    stream_rim = from_behind(grad_streams[: taps - 1], "context", -1)
    stream_ext = jnp.concatenate([grad_streams, stream_rim], 0)
    grad_proj = jnp.zeros((rows, 3, chans), jnp.float32)
    for tap in range(taps):
        grad_proj = grad_proj + short_filter[:, tap][None] * stream_ext[tap : tap + rows]
    grad_proj = grad_proj.astype(jnp.bfloat16)
    short_terms = [
        jnp.sum(grad_streams * proj_ext[taps - 1 - tap : taps - 1 - tap + rows], axis=0)
        for tap in range(taps)
    ]
    short_term = jnp.stack(short_terms, axis=1)
    filters = tree_psum(
        jnp.concatenate([short_term.ravel(), mixer_term.ravel()]), ("dp", "context")
    )
    proj_flat = grad_proj.reshape(rows, 3 * chans)
    in_term = lax.dot_general(
        slab, proj_flat, (((0,), (0,)), ((), ())), preferred_element_type=jnp.float32
    ).reshape(width, 3, chans)
    grad_in, grad_out = (
        lax.psum_scatter(
            in_term.astype(jnp.bfloat16), ("dp", "context"), scatter_dimension=0, tiled=True
        ).astype(jnp.float32),
        lax.psum_scatter(out_term, ("dp", "context"), scatter_dimension=0, tiled=True).T,
    )
    piece = proj_flat
    norm_part = lax.dot_general(
        piece, in_flat, (((1,), (1,)), ((), ())), preferred_element_type=jnp.float32
    ).astype(jnp.bfloat16)
    filters, norm_part = lax.optimization_barrier((filters, norm_part))
    grad_short = filters[: short_term.size].reshape(short_term.shape)
    grad_mixer = filters[short_term.size :].reshape(mixer_term.shape)
    grad_norm = pair_scatter_sum(norm_part)
    grad_x = (
        cotangent[0].astype(jnp.float32)
        + inverse * grad_norm
        - own * inverse**3 * jnp.mean(grad_norm * own, axis=-1, keepdims=True)
    )
    grad_input = grad_x.astype(jnp.bfloat16)[None]
    return (
        block_out,
        grad_input,
        grad_in.astype(jnp.bfloat16),
        grad_out.astype(jnp.bfloat16),
        grad_short,
        grad_mixer,
    )


def solution(mesh):
    devices = mesh.devices
    lead = devices.shape[:2]
    cores = 2
    chips = devices.shape[2] // cores
    mesh = jax.sharding.Mesh(
        devices.reshape(lead + (chips, cores)), ("dp", "context", "tchip", "core")
    )
    placed = (
        P("dp", ("context", "tchip", "core"), None),
        P("dp", None, TENSOR),
        P(TENSOR, "dp"),
        P(None, None, TENSOR),
        P(None, TENSOR),
        P("dp", ("context", "tchip", "core"), None),
    )
    return jax.shard_map(
        per_device,
        mesh=mesh,
        in_specs=placed,
        out_specs=(
            P("dp", ("context", "tchip", "core"), None),
            P("dp", ("context", "tchip", "core"), None),
            P(("dp", "context"), None, TENSOR),
            P(TENSOR, ("dp", "context")),
            P(None, None, TENSOR),
            P(None, TENSOR),
        ),
        check_vma=False,
    )
```

```python
import jax
import jax.numpy as jnp
from jax import lax
from jax.sharding import PartitionSpec as P

EPS = 1e-05
TENSOR = ("tchip", "core")


def from_behind(value, axis, steps):
    count = lax.axis_size(axis)
    initial, last = (max(0, -steps), min(count, count - steps))
    return lax.ppermute(value, axis, [(source, source + steps) for source in range(initial, last)])


def pair_gather(value, axis, dim):
    count = lax.axis_size(axis)
    index = lax.axis_index(axis)
    parts = [value]
    for step in range(1, count):
        parts.append(lax.ppermute(value, axis, [(i, (i + step) % count) for i in range(count)]))
    shape = list(value.shape)
    size = shape[dim]
    shape[dim] = size * count
    full = jnp.zeros(shape, value.dtype)
    for step, part in enumerate(parts):
        start = [0] * len(shape)
        start[dim] = ((index - step) % count) * size
        full = lax.dynamic_update_slice(full, part, start)
    return full


def tree_psum(value, axes):
    for axis in axes:
        count = lax.axis_size(axis)
        if count & (count - 1):
            value = lax.psum(value, axis)
            continue
        step = 1
        while step < count:
            partner = lax.ppermute(value, axis, [(i, i ^ step) for i in range(count)])
            value = value + partner
            step *= 2
    return value


def pair_scatter_sum(value):
    chips = lax.axis_size("tchip")
    cores = lax.axis_size("core")
    rows, width = value.shape
    value = value.reshape(chips, cores, rows // (chips * cores), width)
    pieces = lax.all_to_all(value, "core", 1, 1)
    paired = jnp.sum(pieces.astype(jnp.float32), axis=1).astype(jnp.bfloat16)
    pieces = lax.all_to_all(paired, "tchip", 0, 0)
    return jnp.sum(pieces.astype(jnp.float32), axis=0)


def scatter_sum(value, axis, dim):
    count = lax.axis_size(axis)
    shape = value.shape
    split = shape[:dim] + (count, shape[dim] // count) + shape[dim + 1 :]
    pieces = lax.all_to_all(value.reshape(split), axis, dim, 0)
    return jnp.sum(pieces.astype(jnp.float32), axis=0)


def skew_table(base, span):
    groups = base.shape[0]
    padded = jnp.concatenate([base, jnp.zeros((groups, span + 1), jnp.float32)], axis=1)
    tiled = jnp.tile(padded[:, None, :], (1, span, 1)).reshape(groups, span * (2 * span + 1))
    return tiled[:, : span * 2 * span].reshape(groups, span, 2 * span)


def band_windows(extended, span, groups):
    chans = extended.shape[1]
    padded = jnp.concatenate([extended, jnp.zeros((1, chans), jnp.float32)], 0)
    blocks = padded.shape[0] // span
    padded = padded.reshape(blocks, span, groups, chans // groups)
    return jnp.concatenate([padded[:-1], padded[1:]], axis=1)


def band_apply(table, extended, span):
    groups = table.shape[0]
    chans = extended.shape[1]
    windows = band_windows(extended, span, groups).astype(jnp.bfloat16)
    high = table.astype(jnp.bfloat16)
    low = (table - high.astype(jnp.float32)).astype(jnp.bfloat16)
    result = jnp.einsum(
        "gtu,bugc->btgc", high, windows, preferred_element_type=jnp.float32
    ) + jnp.einsum("gtu,bugc->btgc", low, windows, preferred_element_type=jnp.float32)
    return result.reshape(windows.shape[0] * span, chans)


def band_grad(left, extended, span, groups):
    rows, chans = left.shape
    lhs = left.reshape(rows // span, span, groups, chans // groups)
    windows = band_windows(extended, span, groups).astype(jnp.bfloat16)
    prods = jnp.einsum(
        "btgc,bugc->gtu", lhs.astype(jnp.bfloat16), windows, preferred_element_type=jnp.float32
    )
    flat = jnp.concatenate(
        [prods.reshape(groups, span * 2 * span), jnp.zeros((groups, span), jnp.float32)], axis=1
    )
    skewed = flat.reshape(groups, span, 2 * span + 1).sum(axis=1)
    return jnp.flip(skewed[:, :span], axis=1).T


def short_apply(filters, extended, rows):
    taps = filters.shape[1]
    total = jnp.zeros((rows,) + extended.shape[1:], jnp.float32)
    for tap in range(taps):
        total = total + filters[:, tap][None] * extended[taps - 1 - tap : taps - 1 - tap + rows]
    return total


def per_device(activations, in_weight, out_weight, short_filter, mixer_filter, cotangent):
    rows_own = activations.shape[1]
    width = activations.shape[2]
    rows = rows_own * lax.axis_size("tchip") * lax.axis_size("core")
    span = mixer_filter.shape[0]
    groups = mixer_filter.shape[1]
    taps = short_filter.shape[1]
    chans = short_filter.shape[2]
    own = activations[0].astype(jnp.float32)
    inverse = lax.rsqrt(jnp.mean(own * own, axis=-1, keepdims=True) + EPS)
    normed = (own * inverse).astype(jnp.bfloat16)
    slab = lax.all_gather(normed, TENSOR, axis=0, tiled=True)
    full_in = pair_gather(in_weight, "dp", 0)
    full_out = pair_gather(out_weight, "dp", 1)
    in_flat = full_in.reshape(width, 3 * chans)
    projected = (
        jnp.dot(slab, in_flat, preferred_element_type=jnp.float32)
        .astype(jnp.bfloat16)
        .reshape(rows, 3, chans)
    )
    proj_wide = projected.astype(jnp.float32)
    table_fwd = skew_table(jnp.flip(mixer_filter, axis=0).T, span)
    table_back = skew_table(mixer_filter.T, span)
    wide_rim = from_behind(projected[rows - span - taps + 2 :], "context", 1)
    short_rim = wide_rim[span - 1 :]
    proj_ext = jnp.concatenate([short_rim.astype(jnp.float32), proj_wide], 0)
    streams = short_apply(short_filter, proj_ext, rows)
    gated = (streams[:, 1] * streams[:, 2]).astype(jnp.bfloat16)
    rim_streams = short_apply(short_filter, wide_rim.astype(jnp.float32), span - 1)
    gate_rim = (rim_streams[:, 1] * rim_streams[:, 2]).astype(jnp.bfloat16)
    gate_ext = jnp.concatenate([gate_rim, gated], 0).astype(jnp.float32)
    mixed = band_apply(table_fwd, gate_ext, span)
    output_rows = (streams[:, 0] * mixed).astype(jnp.bfloat16)
    piece = output_rows
    branch = pair_scatter_sum(
        jnp.dot(piece, full_out, preferred_element_type=jnp.float32).astype(jnp.bfloat16)
    )
    cot_slab = lax.all_gather(cotangent[0], TENSOR, axis=0, tiled=True)
    out_term = lax.dot_general(
        cot_slab, output_rows, (((0,), (0,)), ((), ())), preferred_element_type=jnp.float32
    ).astype(jnp.bfloat16)
    out_term, cot_slab = lax.optimization_barrier((out_term, cot_slab))
    grad_rows = lax.dot_general(
        cot_slab, full_out, (((1,), (1,)), ((), ())), preferred_element_type=jnp.float32
    )
    grad_mix = (grad_rows * streams[:, 0]).astype(jnp.bfloat16)
    grad_mix_wide = grad_mix.astype(jnp.float32)
    mix_rim = from_behind(grad_mix[: span - 1], "context", -1)
    per_chan = jnp.repeat(mixer_filter, chans // groups, axis=1)
    head_gate = jnp.stack(
        [jnp.sum(per_chan * grad_mix_wide[t : t + span], axis=0) for t in range(taps - 1)]
    )
    head = slice(0, taps - 1)
    head_streams = jnp.stack(
        [
            grad_rows[head] * mixed[head],
            head_gate * streams[head, 2],
            head_gate * streams[head, 1],
        ],
        axis=1,
    )
    grad_gate = band_apply(
        table_back, jnp.concatenate([grad_mix_wide, mix_rim.astype(jnp.float32)], 0), span
    )
    mixer_term = band_grad(grad_mix_wide, gate_ext, span, groups)
    grad_streams = jnp.stack(
        [grad_rows * mixed, grad_gate * streams[:, 2], grad_gate * streams[:, 1]], axis=1
    )
    branch, grad_streams = lax.optimization_barrier((branch, grad_streams))
    block_out = (own + branch).astype(jnp.bfloat16)[None]
    stream_rim = from_behind(head_streams, "context", -1)
    stream_ext = jnp.concatenate([grad_streams, stream_rim], 0)
    grad_proj = jnp.zeros((rows, 3, chans), jnp.float32)
    for tap in range(taps):
        grad_proj = grad_proj + short_filter[:, tap][None] * stream_ext[tap : tap + rows]
    grad_proj = grad_proj.astype(jnp.bfloat16)
    short_terms = [
        jnp.sum(grad_streams * proj_ext[taps - 1 - tap : taps - 1 - tap + rows], axis=0)
        for tap in range(taps)
    ]
    short_term = jnp.stack(short_terms, axis=1)
    filters = tree_psum(
        jnp.concatenate([short_term.ravel(), mixer_term.ravel()]), ("dp", "context")
    )
    proj_flat = grad_proj.reshape(rows, 3 * chans)
    in_term = lax.dot_general(
        slab, proj_flat, (((0,), (0,)), ((), ())), preferred_element_type=jnp.float32
    ).reshape(width, 3, chans)
    grad_in, grad_out = (
        lax.psum_scatter(
            in_term.astype(jnp.bfloat16), ("dp", "context"), scatter_dimension=0, tiled=True
        ).astype(jnp.float32),
        lax.psum_scatter(out_term, ("dp", "context"), scatter_dimension=0, tiled=True).T,
    )
    piece = proj_flat
    norm_part = lax.dot_general(
        piece, in_flat, (((1,), (1,)), ((), ())), preferred_element_type=jnp.float32
    ).astype(jnp.bfloat16)
    filters, norm_part = lax.optimization_barrier((filters, norm_part))
    grad_short = filters[: short_term.size].reshape(short_term.shape)
    grad_mixer = filters[short_term.size :].reshape(mixer_term.shape)
    grad_norm = pair_scatter_sum(norm_part)
    grad_x = (
        cotangent[0].astype(jnp.float32)
        + inverse * grad_norm
        - own * inverse**3 * jnp.mean(grad_norm * own, axis=-1, keepdims=True)
    )
    grad_input = grad_x.astype(jnp.bfloat16)[None]
    return (
        block_out,
        grad_input,
        grad_in.astype(jnp.bfloat16),
        grad_out.astype(jnp.bfloat16),
        grad_short,
        grad_mixer,
    )


def solution(mesh):
    devices = mesh.devices
    lead = devices.shape[:2]
    cores = 2
    chips = devices.shape[2] // cores
    mesh = jax.sharding.Mesh(
        devices.reshape(lead + (chips, cores)), ("dp", "context", "tchip", "core")
    )
    placed = (
        P("dp", ("context", "tchip", "core"), None),
        P("dp", None, TENSOR),
        P(TENSOR, "dp"),
        P(None, None, TENSOR),
        P(None, TENSOR),
        P("dp", ("context", "tchip", "core"), None),
    )
    return jax.shard_map(
        per_device,
        mesh=mesh,
        in_specs=placed,
        out_specs=(
            P("dp", ("context", "tchip", "core"), None),
            P("dp", ("context", "tchip", "core"), None),
            P(("dp", "context"), None, TENSOR),
            P(TENSOR, ("dp", "context")),
            P(None, None, TENSOR),
            P(None, TENSOR),
        ),
        check_vma=False,
    )
```

```python
import jax
import jax.numpy as jnp
from jax import lax
from jax.sharding import PartitionSpec as P

EPS = 1e-05
TENSOR = ("tchip", "core")


def from_behind(value, axis, steps):
    count = lax.axis_size(axis)
    initial, last = (max(0, -steps), min(count, count - steps))
    return lax.ppermute(value, axis, [(source, source + steps) for source in range(initial, last)])


def pair_gather(value, axis, dim):
    count = lax.axis_size(axis)
    index = lax.axis_index(axis)
    parts = [value]
    for step in range(1, count):
        parts.append(lax.ppermute(value, axis, [(i, (i + step) % count) for i in range(count)]))
    shape = list(value.shape)
    size = shape[dim]
    shape[dim] = size * count
    full = jnp.zeros(shape, value.dtype)
    for step, part in enumerate(parts):
        start = [0] * len(shape)
        start[dim] = ((index - step) % count) * size
        full = lax.dynamic_update_slice(full, part, start)
    return full


def tree_psum(value, axes):
    for axis in axes:
        count = lax.axis_size(axis)
        if count & (count - 1):
            value = lax.psum(value, axis)
            continue
        step = 1
        while step < count:
            partner = lax.ppermute(value, axis, [(i, i ^ step) for i in range(count)])
            value = value + partner
            step *= 2
    return value


def core_sum(value):
    chips = lax.axis_size("tchip")
    cores = lax.axis_size("core")
    rows, width = value.shape
    value = value.reshape(chips, cores, rows // (chips * cores), width)
    pieces = lax.all_to_all(value, "core", 1, 1)
    return jnp.sum(pieces.astype(jnp.float32), axis=1).astype(jnp.bfloat16)


def chip_sum(paired):
    pieces = lax.all_to_all(paired, "tchip", 0, 0)
    return jnp.sum(pieces.astype(jnp.float32), axis=0)


def pair_scatter_sum(value):
    return chip_sum(core_sum(value))


def scatter_sum(value, axis, dim):
    count = lax.axis_size(axis)
    shape = value.shape
    split = shape[:dim] + (count, shape[dim] // count) + shape[dim + 1 :]
    pieces = lax.all_to_all(value.reshape(split), axis, dim, 0)
    return jnp.sum(pieces.astype(jnp.float32), axis=0)


def skew_table(base, span):
    groups = base.shape[0]
    padded = jnp.concatenate([base, jnp.zeros((groups, span + 1), jnp.float32)], axis=1)
    tiled = jnp.tile(padded[:, None, :], (1, span, 1)).reshape(groups, span * (2 * span + 1))
    return tiled[:, : span * 2 * span].reshape(groups, span, 2 * span)


def band_windows(extended, span, groups):
    chans = extended.shape[1]
    padded = jnp.concatenate([extended, jnp.zeros((1, chans), jnp.float32)], 0)
    blocks = padded.shape[0] // span
    padded = padded.reshape(blocks, span, groups, chans // groups)
    return jnp.concatenate([padded[:-1], padded[1:]], axis=1)


def band_apply(table, extended, span):
    groups = table.shape[0]
    chans = extended.shape[1]
    windows = band_windows(extended, span, groups).astype(jnp.bfloat16)
    high = table.astype(jnp.bfloat16)
    low = (table - high.astype(jnp.float32)).astype(jnp.bfloat16)
    result = jnp.einsum(
        "gtu,bugc->btgc", high, windows, preferred_element_type=jnp.float32
    ) + jnp.einsum("gtu,bugc->btgc", low, windows, preferred_element_type=jnp.float32)
    return result.reshape(windows.shape[0] * span, chans)


def band_grad(left, extended, span, groups):
    rows, chans = left.shape
    lhs = left.reshape(rows // span, span, groups, chans // groups)
    windows = band_windows(extended, span, groups).astype(jnp.bfloat16)
    prods = jnp.einsum(
        "btgc,bugc->gtu", lhs.astype(jnp.bfloat16), windows, preferred_element_type=jnp.float32
    )
    flat = jnp.concatenate(
        [prods.reshape(groups, span * 2 * span), jnp.zeros((groups, span), jnp.float32)], axis=1
    )
    skewed = flat.reshape(groups, span, 2 * span + 1).sum(axis=1)
    return jnp.flip(skewed[:, :span], axis=1).T


def short_apply(filters, extended, rows):
    taps = filters.shape[1]
    total = jnp.zeros((rows,) + extended.shape[1:], jnp.float32)
    for tap in range(taps):
        total = total + filters[:, tap][None] * extended[taps - 1 - tap : taps - 1 - tap + rows]
    return total


def per_device(activations, in_weight, out_weight, short_filter, mixer_filter, cotangent):
    rows_own = activations.shape[1]
    width = activations.shape[2]
    rows = rows_own * lax.axis_size("tchip") * lax.axis_size("core")
    span = mixer_filter.shape[0]
    groups = mixer_filter.shape[1]
    taps = short_filter.shape[1]
    chans = short_filter.shape[2]
    own = activations[0].astype(jnp.float32)
    inverse = lax.rsqrt(jnp.mean(own * own, axis=-1, keepdims=True) + EPS)
    normed = (own * inverse).astype(jnp.bfloat16)
    slab = lax.all_gather(normed, TENSOR, axis=0, tiled=True)
    full_in = pair_gather(in_weight, "dp", 0)
    full_out = pair_gather(out_weight, "dp", 1)
    in_flat = full_in.reshape(width, 3 * chans)
    projected = (
        jnp.dot(slab, in_flat, preferred_element_type=jnp.float32)
        .astype(jnp.bfloat16)
        .reshape(rows, 3, chans)
    )
    proj_wide = projected.astype(jnp.float32)
    table_fwd = skew_table(jnp.flip(mixer_filter, axis=0).T, span)
    table_back = skew_table(mixer_filter.T, span)
    wide_rim = from_behind(projected[rows - span - taps + 2 :], "context", 1)
    short_rim = wide_rim[span - 1 :]
    proj_ext = jnp.concatenate([short_rim.astype(jnp.float32), proj_wide], 0)
    streams = short_apply(short_filter, proj_ext, rows)
    gated = (streams[:, 1] * streams[:, 2]).astype(jnp.bfloat16)
    rim_streams = short_apply(short_filter, wide_rim.astype(jnp.float32), span - 1)
    gate_rim = (rim_streams[:, 1] * rim_streams[:, 2]).astype(jnp.bfloat16)
    gate_ext = jnp.concatenate([gate_rim, gated], 0).astype(jnp.float32)
    mixed = band_apply(table_fwd, gate_ext, span)
    output_rows = (streams[:, 0] * mixed).astype(jnp.bfloat16)
    piece = output_rows
    branch = pair_scatter_sum(
        jnp.dot(piece, full_out, preferred_element_type=jnp.float32).astype(jnp.bfloat16)
    )
    cot_slab = lax.all_gather(cotangent[0], TENSOR, axis=0, tiled=True)
    out_term = lax.dot_general(
        cot_slab, output_rows, (((0,), (0,)), ((), ())), preferred_element_type=jnp.float32
    ).astype(jnp.bfloat16)
    out_term, cot_slab = lax.optimization_barrier((out_term, cot_slab))
    grad_rows = lax.dot_general(
        cot_slab, full_out, (((1,), (1,)), ((), ())), preferred_element_type=jnp.float32
    )
    grad_mix = (grad_rows * streams[:, 0]).astype(jnp.bfloat16)
    grad_mix_wide = grad_mix.astype(jnp.float32)
    mix_rim = from_behind(grad_mix[: span - 1], "context", -1)
    grad_gate = band_apply(
        table_back, jnp.concatenate([grad_mix_wide, mix_rim.astype(jnp.float32)], 0), span
    )
    mixer_term = band_grad(grad_mix_wide, gate_ext, span, groups)
    grad_streams = jnp.stack(
        [grad_rows * mixed, grad_gate * streams[:, 2], grad_gate * streams[:, 1]], axis=1
    )
    branch, grad_streams = lax.optimization_barrier((branch, grad_streams))
    block_out = (own + branch).astype(jnp.bfloat16)[None]
    stream_rim = from_behind(grad_streams[: taps - 1], "context", -1)
    stream_ext = jnp.concatenate([grad_streams, stream_rim], 0)
    grad_proj = jnp.zeros((rows, 3, chans), jnp.float32)
    for tap in range(taps):
        grad_proj = grad_proj + short_filter[:, tap][None] * stream_ext[tap : tap + rows]
    grad_proj = grad_proj.astype(jnp.bfloat16)
    short_terms = [
        jnp.sum(grad_streams * proj_ext[taps - 1 - tap : taps - 1 - tap + rows], axis=0)
        for tap in range(taps)
    ]
    short_term = jnp.stack(short_terms, axis=1)
    filters = tree_psum(
        jnp.concatenate([short_term.ravel(), mixer_term.ravel()]), ("dp", "context")
    )
    proj_flat = grad_proj.reshape(rows, 3 * chans)
    in_term = lax.dot_general(
        slab, proj_flat, (((0,), (0,)), ((), ())), preferred_element_type=jnp.float32
    ).reshape(width, 3, chans)
    grad_in, grad_out = (
        lax.psum_scatter(
            in_term.astype(jnp.bfloat16), ("dp", "context"), scatter_dimension=0, tiled=True
        ).astype(jnp.float32),
        lax.psum_scatter(out_term, ("dp", "context"), scatter_dimension=0, tiled=True).T,
    )
    piece = proj_flat
    norm_part = lax.dot_general(
        piece, in_flat, (((1,), (1,)), ((), ())), preferred_element_type=jnp.float32
    ).astype(jnp.bfloat16)
    norm_part = core_sum(norm_part)
    filters, norm_part = lax.optimization_barrier((filters, norm_part))
    grad_short = filters[: short_term.size].reshape(short_term.shape)
    grad_mixer = filters[short_term.size :].reshape(mixer_term.shape)
    grad_norm = chip_sum(norm_part)
    grad_x = (
        cotangent[0].astype(jnp.float32)
        + inverse * grad_norm
        - own * inverse**3 * jnp.mean(grad_norm * own, axis=-1, keepdims=True)
    )
    grad_input = grad_x.astype(jnp.bfloat16)[None]
    return (
        block_out,
        grad_input,
        grad_in.astype(jnp.bfloat16),
        grad_out.astype(jnp.bfloat16),
        grad_short,
        grad_mixer,
    )


def solution(mesh):
    devices = mesh.devices
    lead = devices.shape[:2]
    cores = 2
    chips = devices.shape[2] // cores
    mesh = jax.sharding.Mesh(
        devices.reshape(lead + (chips, cores)), ("dp", "context", "tchip", "core")
    )
    placed = (
        P("dp", ("context", "tchip", "core"), None),
        P("dp", None, TENSOR),
        P(TENSOR, "dp"),
        P(None, None, TENSOR),
        P(None, TENSOR),
        P("dp", ("context", "tchip", "core"), None),
    )
    return jax.shard_map(
        per_device,
        mesh=mesh,
        in_specs=placed,
        out_specs=(
            P("dp", ("context", "tchip", "core"), None),
            P("dp", ("context", "tchip", "core"), None),
            P(("dp", "context"), None, TENSOR),
            P(TENSOR, ("dp", "context")),
            P(None, None, TENSOR),
            P(None, TENSOR),
        ),
        check_vma=False,
    )
```
